32 devices in a mesh: section: 2 (over x), seq: 16 (over z, y, core).
Axes of the slice: x: 2, y: 2, z: 4, core: 2. Of those that a mesh axis runs over, the one named last changes fastest.
Arguments:
- prev_out: bfloat16 [2, 2048, 1792], P('section', 'seq'), may hold values from -6 to 6
- prev_grad: bfloat16 [2, 2048, 1792], P('section', 'seq'), may hold values from -6 to 6
- saved_in: bfloat16 [2, 2048, 1792], P('section', 'seq'), may hold values from -6 to 6
- seq_mix: bfloat16 [2, 128, 128], P('section'), may hold values from -0.5 to 0.5
- coeffs: float32 [2, 4, 4, 1792], P('section'), may hold values from -1 to 1
- mixer: bfloat16 [2, 1792, 448], P('section'), may hold values from -0.25 to 0.25
Outputs:
- out_fwd: bfloat16 [2, 2048, 1792], P('section', 'seq')
- out_dh: bfloat16 [2, 2048, 1792], P('section', 'seq')
- grad_w: float32 [2, 1792, 448], P('section', 'seq')
- grad_b: float32 [2, 128, 128], P('section')
The draws below stay inside these ranges and needn't reach their ends.
All inputs are finite; a program needn't handle non-finite values.
Results may differ from the reference program's by a relative error of at most 0.01.
Values may be sent and summed in bfloat16 or wider, within the bound.
No kernel may reach another device: no remote copies, remote signals or barrier semaphores. Data moves between devices by JAX's collectives and lax.ppermute only.
A program may use at most 64 MiB of HBM per device.

```python
import jax
import jax.numpy as jnp

D = 1792
NBLK = 4
SEQBLK = 128
S_DEV = 128
BD = 448
SECTIONS = 2
TOKENS = 2048
LEVELS = 4
N_SEQ = 16


def spiked(values, own_key, source, target, parts, factor):
    def block_of(position):
        return (jnp.arange(values.shape[position]) // (values.shape[position] // parts)).reshape((-1,) + (1,) * (values.ndim - 1 - position))

    near = jax.random.permutation(own_key, parts)[block_of(target)]
    second = (block_of(target) + parts // 2) % parts
    return jnp.where((block_of(source) == near) | (block_of(source) == second), factor * values, values)


def block_levels(own_key, dims, pieces, least, top_value):
    def one(dim, blocks):
        draws = jax.random.uniform(jax.random.fold_in(jax.random.fold_in(own_key, 6), dim), (blocks,), jnp.float32, least / len(pieces), top_value / len(pieces))
        return jnp.repeat(jnp.exp(draws), dims[dim] // blocks).reshape((-1,) + (1,) * (len(dims) - dim - 1))

    gain = one(*pieces[0])
    for cut in pieces[1:]:
        gain = gain * one(*cut)
    return gain


def centred(stream_key, shape, scale, reach, pieces=(), kind=jnp.bfloat16):
    array = jax.random.normal(stream_key, shape, jnp.float32) * scale
    if len(pieces) > 0:
        array = block_levels(stream_key, shape, pieces, -0.22, 0.18) * array
    return jnp.clip(array, min=-reach, max=reach).astype(kind)


def heavy_noise(own_key, dims, deviation, limit, pieces, heavy, held_as=jnp.bfloat16):
    values = deviation * jax.random.normal(own_key, dims, jnp.float32)
    if pieces:
        values = values * block_levels(own_key, dims, pieces, -0.22, 0.18)
    return jnp.clip(spiked(values, jax.random.fold_in(own_key, 3), *heavy), -limit, limit).astype(held_as)


def setup_inputs(seed: int = 0) -> dict:
    key_of = jax.random.split(jax.random.key(seed), 7)
    return {
        "prev_out": centred(key_of[0], (SECTIONS, TOKENS, D), 1.0, 6.0, ((0, 2), (1, 16))),
        "prev_grad": centred(key_of[1], (SECTIONS, TOKENS, D), 1.0, 6.0, ((0, 2), (1, 16))),
        "saved_in": heavy_noise(key_of[2], (SECTIONS, TOKENS, D), 1.0, 6.0, ((0, 2), (1, 16)), (1, 2, 16, 2.0)),
        "seq_mix": centred(key_of[3], (SECTIONS, SEQBLK, SEQBLK), SEQBLK ** -0.5, 0.5, ((0, 2),)),
        "coeffs": jnp.clip(jax.random.uniform(key_of[4], (SECTIONS, LEVELS, 4, D), jnp.float32, -1.0, 1.0) * block_levels(key_of[4], (SECTIONS, LEVELS, 4, D), ((0, 2),), -0.4, 0.0), -1.0, 1.0),
        "mixer": centred(key_of[5], (SECTIONS, D, BD), BD ** -0.5, 0.25, ((0, 2),)),
    }


def block_mix(rows, blocks):
    shaped = rows.reshape(-1, SEQBLK, D).astype(jnp.float32)
    mixed = jnp.einsum('ij,bjd->bid', blocks.astype(jnp.float32), shaped)
    return mixed.reshape(-1, D).astype(jnp.bfloat16)


def butterfly(state, factors):
    current = state.reshape(N_SEQ, S_DEV, D)
    for bit_level in range(LEVELS):
        span = 2 ** bit_level
        paired = current.reshape(N_SEQ // (2 * span), 2, span, S_DEV, D).astype(jnp.float32)
        lower = paired[:, 0]
        upper = paired[:, 1]
        new_lower = factors[bit_level, 0] * lower + factors[bit_level, 1] * upper
        new_upper = factors[bit_level, 2] * lower + factors[bit_level, 3] * upper
        current = jnp.stack([new_lower, new_upper], axis=1).astype(jnp.bfloat16).reshape(N_SEQ, S_DEV, D)
    return current.reshape(-1, D)


def butterfly_adjoint(state, factors):
    current = state.reshape(N_SEQ, S_DEV, D)
    for bit_level in reversed(range(LEVELS)):
        span = 2 ** bit_level
        paired = current.reshape(N_SEQ // (2 * span), 2, span, S_DEV, D).astype(jnp.float32)
        lower = paired[:, 0]
        upper = paired[:, 1]
        new_lower = factors[bit_level, 0] * lower + factors[bit_level, 2] * upper
        new_upper = factors[bit_level, 1] * lower + factors[bit_level, 3] * upper
        current = jnp.stack([new_lower, new_upper], axis=1).astype(jnp.bfloat16).reshape(N_SEQ, S_DEV, D)
    return current.reshape(-1, D)


def layer_forward(rows, blocks, factors, weights):
    blocked = block_mix(rows, blocks)
    state = butterfly(blocked, factors)
    act = (rows.astype(jnp.float32) + state.astype(jnp.float32)).astype(jnp.bfloat16)
    act3 = act.reshape(-1, NBLK, BD)
    weight3 = weights.reshape(NBLK, BD, BD)
    pre = jnp.einsum('tbi,bio->tbo', act3.astype(jnp.float32), weight3.astype(jnp.float32))
    return act3, pre


def reference(prev_out, prev_grad, saved_in, seq_mix, coeffs, mixer):
    fwd_list, dh_list, gw_list, gb_list = [], [], [], []
    for section in range(SECTIONS):
        blocks = seq_mix[section]
        factors = coeffs[section]
        weights = mixer[section]
        incoming = prev_out[(section - 1) % SECTIONS]
        upstream = prev_grad[(section + 1) % SECTIONS]
        act3, pre = layer_forward(incoming, blocks, factors, weights)
        result = (act3.astype(jnp.float32) + jax.nn.silu(pre)).reshape(-1, D).astype(jnp.bfloat16)
        fwd_list.append(result)
        stored = saved_in[section]
        act_two, pre_two = layer_forward(stored, blocks, factors, weights)
        sigma = jax.nn.sigmoid(pre_two)
        gz = (upstream.astype(jnp.float32).reshape(-1, NBLK, BD) * (sigma * (1.0 + pre_two * (1.0 - sigma)))).astype(jnp.bfloat16)
        weight3 = weights.reshape(NBLK, BD, BD)
        back = jnp.einsum('tbo,bio->tbi', gz.astype(jnp.float32), weight3.astype(jnp.float32))
        d_act = (upstream.astype(jnp.float32) + back.reshape(-1, D)).astype(jnp.bfloat16)
        grad_weight = jnp.einsum('tbi,tbo->bio', act_two.astype(jnp.float32), gz.astype(jnp.float32)).reshape(D, BD)
        gw_list.append(grad_weight)
        dblocked = butterfly_adjoint(d_act, factors)
        dblk = dblocked.reshape(-1, SEQBLK, D).astype(jnp.float32)
        stored_blk = stored.reshape(-1, SEQBLK, D).astype(jnp.float32)
        gb_list.append(jnp.einsum('bid,bjd->ij', dblk, stored_blk))
        through = jnp.einsum('ij,bid->bjd', blocks.astype(jnp.float32), dblk).reshape(-1, D)
        dh_list.append((d_act.astype(jnp.float32) + through).astype(jnp.bfloat16))
    return jnp.stack(fwd_list), jnp.stack(dh_list), jnp.stack(gw_list), jnp.stack(gb_list)
```

```python
import functools

import jax
import jax.numpy as jnp
from jax import lax
from jax.experimental import pallas as pl
from jax.experimental.pallas import tpu as pltpu
from jax.sharding import PartitionSpec as P

F32 = jnp.float32
BF16 = jnp.bfloat16
VMEM = pl.BlockSpec(memory_space=pltpu.VMEM)
SMEM = pl.BlockSpec(memory_space=pltpu.SMEM)


def dot(a, b, ca, cb):
    return lax.dot_general(a, b, (((ca,), (cb,)), ((), ())), preferred_element_type=F32)


def call(body, outs, ins, scratch=(), name=None):
    return pl.pallas_call(
        body,
        out_shape=outs,
        in_specs=[SMEM if a.dtype == jnp.int32 else VMEM for a in ins],
        out_specs=jax.tree.map(lambda _: VMEM, outs),
        scratch_shapes=scratch,
        name=name,
    )(*ins)


def pack_body(nb, z_ref, x_ref, *refs):
    outs, buf = refs[:nb], refs[nb]
    rows, width = x_ref.shape
    bw = width // nb
    for j in range(width // 128):
        buf[j * 128 : (j + 1) * 128, :] = x_ref[:, j * 128 : (j + 1) * 128].T
    z = z_ref[0]
    for k in range(nb):
        start = pl.multiple_of(jnp.bitwise_xor(z, k) * bw, 16)
        outs[k][...] = buf[pl.ds(start, bw), :]


def pack(z, x, nb, name):
    rows, width = x.shape
    bw = width // nb
    return call(
        functools.partial(pack_body, nb),
        [jax.ShapeDtypeStruct((bw, rows), x.dtype)] * nb,
        [z, x],
        [pltpu.VMEM((width, rows), x.dtype)],
        name,
    )


def unpack_body(nb, z_ref, *refs):
    ins, out, buf = refs[:nb], refs[nb], refs[nb + 1]
    rows, width = out.shape
    bw = width // nb
    z = z_ref[0]
    for k in range(nb):
        start = pl.multiple_of(jnp.bitwise_xor(z, k) * bw, 16)
        buf[pl.ds(start, bw), :] = ins[k][...]
    for j in range(width // 128):
        out[:, j * 128 : (j + 1) * 128] = buf[j * 128 : (j + 1) * 128, :].T


def unpack(z, pieces, name):
    nb = len(pieces)
    bw, rows = pieces[0].shape
    return call(
        functools.partial(unpack_body, nb),
        jax.ShapeDtypeStruct((rows, nb * bw), pieces[0].dtype),
        [z, *pieces],
        [pltpu.VMEM((nb * bw, rows), pieces[0].dtype)],
        name,
    )


def local_levels(vals, coef, first):
    vals = list(vals)
    nb = len(vals)
    for j in range(nb.bit_length() - 1):
        c = [coef[:, first + 4 * j + i : first + 4 * j + i + 1] for i in range(4)]
        for k in range(nb):
            if not k >> j & 1:
                m = k | 1 << j
                a, b = vals[k], vals[m]
                vals[k] = c[0] * a + c[1] * b
                vals[m] = c[2] * b + c[3] * a
    return vals


CH = 64


def local_body(nb, first, coef_ref, *refs):
    ins, out = refs[:nb], refs[nb]
    for s in range(0, out.shape[1], CH):
        vals = [r[s : s + CH, :].astype(F32) for r in ins]
        vals = local_levels(vals, coef_ref[s : s + CH, :], first)
        for k in range(nb):
            out[k, s : s + CH, :] = vals[k].astype(BF16)


def combine_body(first, coef_ref, own_ref, other_ref, out_ref):
    for s in range(0, out_ref.shape[1], CH):
        c0 = coef_ref[s : s + CH, first : first + 1]
        c1 = coef_ref[s : s + CH, first + 1 : first + 2]
        for k in range(out_ref.shape[0]):
            out_ref[k, s : s + CH, :] = (
                c0 * own_ref[k, s : s + CH, :].astype(F32) + c1 * other_ref[k, s : s + CH, :].astype(F32)
            ).astype(BF16)


def combine(coef, first, own, other, name):
    return call(
        functools.partial(combine_body, first),
        jax.ShapeDtypeStruct(own.shape, BF16),
        [coef, own, other],
        (),
        name,
    )


def forward_body(nb, first, coef_ref, b_ref, wt_ref, own_ref, other_ref, *refs):
    ins, outs = refs[:nb], refs[nb : 2 * nb]
    c0 = coef_ref[:, first : first + 1]
    c1 = coef_ref[:, first + 1 : first + 2]
    for k in range(nb):
        u = (c0 * own_ref[k].astype(F32) + c1 * other_ref[k].astype(F32)).astype(BF16)
        act = (ins[k][...].astype(F32) + dot(u, b_ref[...], 1, 1)).astype(BF16)
        pre = dot(wt_ref[...], act, 1, 0)
        outs[k][...] = (act.astype(F32) + pre * jax.nn.sigmoid(pre)).astype(BF16)


def backward_body(nb, first, first_adj, coef_ref, b_ref, w_ref, wt_ref, own_ref, other_ref, *refs):
    ins, ups = refs[:nb], refs[nb : 2 * nb]
    v_ref, d_ref, act_ref, gz_ref, u_ref = refs[2 * nb :]
    c0 = coef_ref[:, first : first + 1]
    c1 = coef_ref[:, first + 1 : first + 2]
    vs = []
    for k in range(nb):
        u = (c0 * own_ref[k].astype(F32) + c1 * other_ref[k].astype(F32)).astype(BF16)
        u_ref[k] = u
        act = (ins[k][...].astype(F32) + dot(u, b_ref[...], 1, 1)).astype(BF16)
        act_ref[k] = act
        pre = dot(wt_ref[...], act, 1, 0)
        sig = jax.nn.sigmoid(pre)
        up = ups[k][...].astype(F32)
        gz = (up * (sig * (1.0 + pre * (1.0 - sig)))).astype(BF16)
        gz_ref[k] = gz
        d = (up + dot(w_ref[...], gz, 1, 0)).astype(BF16)
        d_ref[k] = d
        vs.append(dot(d, b_ref[...], 1, 0))
    vs = local_levels(vs, coef_ref[...], first_adj)
    for k in range(nb):
        v_ref[k] = vs[k].astype(BF16)


def grads_body(nb, act_ref, gz_ref, d_ref, u_ref, gw_ref, gb_ref):
    gw, gb = 0.0, 0.0
    for k in range(nb):
        gw = gw + dot(act_ref[k], gz_ref[k], 1, 1)
        gb = gb + dot(d_ref[k], u_ref[k], 0, 0)
    gw_ref[...] = gw
    gb_ref[...] = gb


def finish_body(nb, first, coef_ref, own_ref, other_ref, d_ref, *outs):
    for s in range(0, own_ref.shape[1], CH):
        c0 = coef_ref[s : s + CH, first : first + 1]
        c1 = coef_ref[s : s + CH, first + 1 : first + 2]
        for k in range(nb):
            outs[k][s : s + CH, :] = (
                d_ref[k, s : s + CH, :].astype(F32)
                + c0 * own_ref[k, s : s + CH, :].astype(F32)
                + c1 * other_ref[k, s : s + CH, :].astype(F32)
            ).astype(BF16)


def on_device(prev_out, prev_grad, saved_in, seq_mix, coeffs, mixer):
    n_sec, n_seq = lax.axis_size("section"), lax.axis_size("seq")
    weights = mixer[0]
    width, bw = weights.shape
    nb = width // bw
    low = n_seq // nb
    levels = n_seq.bit_length() - 1
    n_low = low.bit_length() - 1
    q = lax.axis_index("seq")
    col = q // low
    z = col.astype(jnp.int32).reshape(1)
    blocks = seq_mix[0]
    rows = prev_out.shape[1]

    def send(x, shift, flip):
        pairs = [
            (s * n_seq + i, (s + shift) % n_sec * n_seq + (i ^ flip)) for s in range(n_sec) for i in range(n_seq)
        ]
        return lax.ppermute(x, ("section", "seq"), pairs)

    cf = lax.dynamic_slice_in_dim(coeffs[0], col * bw, bw, 2)
    bits = [jnp.bitwise_and(jnp.right_shift(q, l), 1) == 1 for l in range(levels)]

    def table(order_lower, order_upper, l):
        return jnp.where(bits[l], cf[l, jnp.array(order_upper)], cf[l, jnp.array(order_lower)])

    cols = []
    for l in range(n_low, levels):
        cols.append(table([0, 1, 3, 2], [3, 2, 0, 1], l))
    for l in range(n_low):
        cols.append(table([0, 1], [3, 2], l))
    for l in range(n_low, levels):
        cols.append(table([0, 2, 3, 1], [3, 1, 0, 2], l))
    for l in range(n_low):
        cols.append(table([0, 2], [3, 1], l))
    coef = jnp.concatenate(cols, 0).T
    n_top = levels - n_low
    fwd_loc, fwd_low = 0, 4 * n_top
    adj_loc = fwd_low + 2 * n_low
    adj_low = adj_loc + 4 * n_top

    w_block = lax.dynamic_slice_in_dim(weights, col * bw, bw, 0)
    w_block_t = w_block.T

    def stacked(n):
        return jax.ShapeDtypeStruct((n, bw, rows), BF16)

    def spread(pieces, name):
        u = call(functools.partial(local_body, nb, fwd_loc), stacked(nb), [coef, *pieces], (), name)
        for l in range(n_low):
            other = send(u, 0, 1 << l)
            if l == n_low - 1:
                return u, other
            u = combine(coef, fwd_low + 2 * l, u, other, name + "_mix")

    f_last = fwd_low + 2 * (n_low - 1)

    piece = jax.ShapeDtypeStruct((bw, rows), BF16)
    fp = pack(z, prev_out[0], nb, "pack_f")
    fr = [send(fp[k], 1, k * low) for k in range(nb)]
    sp = pack(z, saved_in[0], nb, "pack_s")
    sr = [sp[0]] + [send(sp[k], 0, k * low) for k in range(1, nb)]
    up = pack(z, prev_grad[0], nb, "pack_u")
    ur = [send(up[k], -1, k * low) for k in range(nb)]

    f_own, f_other = spread(fr, "levels_f")
    s_own, s_other = spread(sr, "levels_s")
    fo = call(
        functools.partial(forward_body, nb, f_last),
        [piece] * nb,
        [coef, blocks, w_block_t, f_own, f_other, *fr],
        (),
        "layer_f",
    )
    fo = [fo[0]] + [send(fo[k], 0, k * low) for k in range(1, nb)]

    v, d, act, gz, u = call(
        functools.partial(backward_body, nb, f_last, adj_loc),
        [stacked(nb)] * 5,
        [coef, blocks, w_block, w_block_t, s_own, s_other, *sr, *ur],
        (),
        "layer_b",
    )
    for l in range(n_low):
        other = send(v, 0, 1 << l)
        if l < n_low - 1:
            v = combine(coef, adj_low + 2 * l, v, other, "adjoint_mix")
    gw, gb = call(
        functools.partial(grads_body, nb),
        [jax.ShapeDtypeStruct((bw, bw), F32), jax.ShapeDtypeStruct((rows, rows), F32)],
        [act, gz, d, u],
        (),
        "weight_grads",
    )
    do = call(
        functools.partial(finish_body, nb, adj_low + 2 * (n_low - 1)),
        [piece] * nb,
        [coef, v, other, d],
        (),
        "finish_b",
    )
    do = [do[0]] + [send(do[k], 0, k * low) for k in range(1, nb)]

    for l in range(n_low):
        half = gw.reshape(low >> l + 1, 2, bw // low, bw)
        mine = jnp.where(bits[l], half[:, 1], half[:, 0])
        theirs = jnp.where(bits[l], half[:, 0], half[:, 1]).astype(BF16)
        gw = mine + send(theirs, 0, 1 << l).astype(F32)
    grad_w = gw.reshape(bw // low, bw)
    for l in range(levels):
        gb = gb + send(gb, 0, 1 << l)
    out_f = unpack(z, fo, "unpack_f")
    out_d = unpack(z, do, "unpack_b")
    return out_f[None], out_d[None], grad_w[None], gb[None]


def solution(mesh):
    placed = (
        P("section", "seq", None),
        P("section", "seq", None),
        P("section", "seq", None),
        P("section", None, None),
        P("section", None, None, None),
        P("section", None, None),
    )
    return jax.shard_map(
        on_device,
        mesh=mesh,
        in_specs=placed,
        out_specs=(
            P("section", "seq", None),
            P("section", "seq", None),
            P("section", "seq", None),
            P("section", None, None),
        ),
        check_vma=False,
    )
```

```python
import functools

import jax
import jax.numpy as jnp
from jax import lax
from jax.experimental import pallas as pl
from jax.experimental.pallas import tpu as pltpu
from jax.sharding import PartitionSpec as P

F32 = jnp.float32
BF16 = jnp.bfloat16
LANES = 128
CH = 64


def dot(a, b, ca, cb):
    return lax.dot_general(a, b, (((ca,), (cb,)), ((), ())), preferred_element_type=F32)


def near_memory(x):
    return pltpu.with_memory_space_constraint(x, pltpu.VMEM)


def call(body, outs, ins, scratch=(), name=None, deps=(), out_hbm=False):
    n_in, n_dep = len(ins), len(deps)

    def kernel(*refs):
        body(*refs[:n_in], *refs[n_in + n_dep :])

    specs = []
    args = []
    for a in ins:
        if a.dtype == jnp.int32:
            specs.append(pl.BlockSpec(memory_space=pltpu.SMEM))
            args.append(a)
        else:
            specs.append(pl.BlockSpec(memory_space=pltpu.VMEM))
            args.append(near_memory(a))
    for a in deps:
        specs.append(pl.BlockSpec(memory_space=pl.ANY))
        args.append(a)
    shapes = jax.tree.map(
        lambda o: o if out_hbm else pltpu.VMEM(o.shape, o.dtype),
        outs,
    )
    return pl.pallas_call(
        kernel,
        out_shape=shapes,
        in_specs=specs,
        out_specs=jax.tree.map(lambda _: pl.BlockSpec(memory_space=pltpu.VMEM), outs),
        scratch_shapes=scratch,
        name=name,
        compiler_params=pltpu.CompilerParams(vmem_limit_bytes=16 << 20),
        cost_estimate=pl.CostEstimate(flops=1000, bytes_accessed=1000, transcendentals=0),
    )(*args)


def shape(*dims, dtype=BF16):
    return jax.ShapeDtypeStruct(dims, dtype)


def pack_body(nb, at_ref, x_ref, *refs):
    outs, buf = refs[:nb], refs[nb]
    width = x_ref.shape[1]
    bw = width // nb
    for j in range(0, width, LANES):
        buf[j : j + LANES, :] = x_ref[:, j : j + LANES].T
    for k in range(nb):
        start = pl.multiple_of(jnp.bitwise_xor(at_ref[0], k) * bw, 16)
        outs[k][...] = buf[pl.ds(start, bw), :]


def unpack_body(nb, at_ref, *refs):
    ins, out, buf = refs[:nb], refs[nb], refs[nb + 1]
    width = out.shape[1]
    bw = width // nb
    for k in range(nb):
        start = pl.multiple_of(jnp.bitwise_xor(at_ref[0], k) * bw, 16)
        buf[pl.ds(start, bw), :] = ins[k][...]
    for j in range(0, width, LANES):
        out[:, j : j + LANES] = buf[j : j + LANES, :].T


def prep_body(nb, n_low, at_ref, c_ref, w_ref, coef_ref, wo_ref, wt_ref, buf):
    levels, _, width = c_ref.shape
    bw = width // nb
    for l in range(levels):
        for j in range(0, width, LANES):
            buf[j : j + LANES, 4 * l : 4 * l + 4] = c_ref[l, :, j : j + LANES].T
    start = pl.multiple_of(at_ref[0] * bw, 16)
    cf = buf[pl.ds(start, bw), :]
    col = 0
    for lower, upper, span in (
        ((0, 1, 3, 2), (3, 2, 0, 1), range(n_low, levels)),
        ((0, 1), (3, 2), range(n_low)),
        ((0, 2, 3, 1), (3, 1, 0, 2), range(n_low, levels)),
        ((0, 2), (3, 1), range(n_low)),
    ):
        for l in span:
            for a, b in zip(lower, upper):
                high = at_ref[1 + l] == 1
                coef_ref[:, col : col + 1] = jnp.where(
                    high, cf[:, 4 * l + b : 4 * l + b + 1], cf[:, 4 * l + a : 4 * l + a + 1]
                )
                col += 1
    w = w_ref[pl.ds(start, bw), :]
    wo_ref[...] = w
    wt_ref[...] = w.T


def stack_body(*refs):
    out = refs[-1]
    for k, r in enumerate(refs[:-1]):
        out[k] = r[...]


def pair(coef_ref, first, s):
    return (coef_ref[s : s + CH, first : first + 1], coef_ref[s : s + CH, first + 1 : first + 2])


def combine_body(first, coef_ref, own_ref, other_ref, out_ref):
    for s in range(0, out_ref.shape[1], CH):
        c0, c1 = pair(coef_ref, first, s)
        for k in range(out_ref.shape[0]):
            own = own_ref[k, s : s + CH, :].astype(F32)
            other = other_ref[k, s : s + CH, :].astype(F32)
            out_ref[k, s : s + CH, :] = (c0 * own + c1 * other).astype(BF16)


def local_levels(vals, coef, first):
    vals = list(vals)
    nb = len(vals)
    for j in range(nb.bit_length() - 1):
        c = [coef[:, first + 4 * j + i : first + 4 * j + i + 1] for i in range(4)]
        for k in range(nb):
            if not k >> j & 1:
                m = k | 1 << j
                a, b = vals[k], vals[m]
                vals[k] = c[0] * a + c[1] * b
                vals[m] = c[2] * b + c[3] * a
    return vals


def finish_state(first, loc, coef_ref, chunks, u_ref):
    for s in range(0, u_ref.shape[1], CH):
        c0, c1 = pair(coef_ref, first, s)
        vals = []
        for own_ref, other_ref in chunks:
            for k in range(own_ref.shape[0]):
                vals.append(c0 * own_ref[k, s : s + CH, :].astype(F32) + c1 * other_ref[k, s : s + CH, :].astype(F32))
        vals = local_levels(vals, coef_ref[s : s + CH, :], loc)
        for k, v in enumerate(vals):
            u_ref[k, s : s + CH, :] = v.astype(BF16)


def forward_body(nb, first, loc, coef_ref, b_ref, wt_ref, o0, x0, o1, x1, *refs):
    ins, outs, u_ref = refs[:nb], refs[nb : 2 * nb], refs[2 * nb]
    finish_state(first, loc, coef_ref, ((o0, x0), (o1, x1)), u_ref)
    for k in range(nb):
        act = (ins[k][...].astype(F32) + dot(u_ref[k], b_ref[...], 1, 1)).astype(BF16)
        pre = dot(wt_ref[...], act, 1, 0)
        outs[k][...] = (act.astype(F32) + pre * jax.nn.sigmoid(pre)).astype(BF16)


def backward_body(nb, first, loc, adj, coef_ref, b_ref, w_ref, wt_ref, o0, x0, o1, x1, *refs):
    ins, ups = refs[:nb], refs[nb : 2 * nb]
    v0_ref, v1_ref, d_ref, act_ref, gz_ref, u_ref, v_ref = refs[2 * nb :]
    finish_state(first, loc, coef_ref, ((o0, x0), (o1, x1)), u_ref)
    for k in range(nb):
        act = (ins[k][...].astype(F32) + dot(u_ref[k], b_ref[...], 1, 1)).astype(BF16)
        act_ref[k] = act
        pre = dot(wt_ref[...], act, 1, 0)
        sig = jax.nn.sigmoid(pre)
        up = ups[k][...].astype(F32)
        gz = (up * (sig * (1.0 + pre * (1.0 - sig)))).astype(BF16)
        gz_ref[k] = gz
        d = (up + dot(w_ref[...], gz, 1, 0)).astype(BF16)
        d_ref[k] = d
        v_ref[k] = dot(d, b_ref[...], 1, 0)
    half = nb // 2
    for s in range(0, d_ref.shape[1], CH):
        vals = local_levels([v_ref[k, s : s + CH, :] for k in range(nb)], coef_ref[s : s + CH, :], adj)
        for k in range(half):
            v0_ref[k, s : s + CH, :] = vals[k].astype(BF16)
            v1_ref[k, s : s + CH, :] = vals[half + k].astype(BF16)


def finish_body(k0, n, first, coef_ref, own_ref, other_ref, d_ref, *outs):
    for s in range(0, own_ref.shape[1], CH):
        c0, c1 = pair(coef_ref, first, s)
        for k in range(n):
            outs[k][s : s + CH, :] = (
                d_ref[k0 + k, s : s + CH, :].astype(F32)
                + c0 * own_ref[k, s : s + CH, :].astype(F32)
                + c1 * other_ref[k, s : s + CH, :].astype(F32)
            ).astype(BF16)


def halve(at_ref, l, src, keep_ref, send_ref):
    bit = at_ref[1 + l]
    for j in range(keep_ref.shape[0]):
        keep_ref[j] = src[2 * j + bit]
        send_ref[j] = src[2 * j + 1 - bit].astype(BF16)


def grads_body(nb, at_ref, act_ref, gz_ref, d_ref, u_ref, keep_ref, send_ref, gb_ref, buf):
    gw, gb = 0.0, 0.0
    for k in range(nb):
        gw = gw + dot(act_ref[k], gz_ref[k], 1, 1)
        gb = gb + dot(d_ref[k], u_ref[k], 0, 0)
    gb_ref[...] = gb
    part = buf.shape[1]
    for n in range(buf.shape[0]):
        buf[n] = gw[n * part : (n + 1) * part, :]
    halve(at_ref, 0, buf, keep_ref, send_ref)


def halve_body(l, at_ref, own_ref, other_ref, keep_ref, send_ref, buf):
    buf[...] = own_ref[...] + other_ref[...].astype(F32)
    halve(at_ref, l, buf, keep_ref, send_ref)


def add_body(own_ref, other_ref, out_ref):
    out_ref[...] = own_ref[...] + other_ref[...].astype(F32)


def on_device(prev_out, prev_grad, saved_in, seq_mix, coeffs, mixer):
    n_sec, n_seq = lax.axis_size("section"), lax.axis_size("seq")
    weights = mixer[0]
    width, bw = weights.shape
    nb = width // bw
    low = n_seq // nb
    levels = n_seq.bit_length() - 1
    n_low = low.bit_length() - 1
    n_top = levels - n_low
    q = lax.axis_index("seq").astype(jnp.int32)
    at = jnp.stack([q // low] + [jnp.bitwise_and(jnp.right_shift(q, l), 1) for l in range(levels)])
    blocks = seq_mix[0]
    rows = prev_out.shape[1]
    half = nb // 2
    fwd_loc, fwd_low = 0, 4 * n_top
    adj_loc = fwd_low + 2 * n_low
    adj_low = adj_loc + 4 * n_top
    n_coef = adj_low + 2 * n_low

    def send(x, shift, flip):
        pairs = [
            (s * n_seq + i, (s + shift) % n_sec * n_seq + (i ^ flip)) for s in range(n_sec) for i in range(n_seq)
        ]
        return lax.ppermute(x, ("section", "seq"), pairs)

    def pack(x, name, deps=()):
        return call(
            functools.partial(pack_body, nb),
            [shape(bw, rows)] * nb,
            [at, x],
            [pltpu.VMEM((width, rows), BF16)],
            name,
            deps,
        )

    def unpack(pieces, name):
        return call(
            functools.partial(unpack_body, nb),
            shape(rows, width),
            [at, *pieces],
            [pltpu.VMEM((width, rows), BF16)],
            name,
            (),
            True,
        )

    def exchange(u, first, name):
        for l in range(n_low):
            other = send(u, 0, 1 << l)
            if l < n_low - 1:
                u = call(
                    functools.partial(combine_body, first + 2 * l), shape(*u.shape), [coef, u, other], (), name
                )
        return u, other

    far_first = list(range(nb - 1, -1, -1))

    fp = pack(prev_out[0], "pack_f")
    fr = {k: send(fp[k], 1, k * low) for k in far_first}
    sp = pack(saved_in[0], "pack_s", [fp[0]])
    sr = {k: send(sp[k], 0, k * low) for k in far_first[:-1]}
    sr[0] = sp[0]
    up = pack(prev_grad[0], "pack_u", [sp[0]])
    ur = {k: send(up[k], -1, k * low) for k in far_first}

    coef, w_own, w_own_t = call(
        functools.partial(prep_body, nb, n_low),
        [shape(bw, n_coef, dtype=F32), shape(bw, bw), shape(bw, bw)],
        [at, coeffs[0], weights],
        [pltpu.VMEM((width, 4 * levels), F32)],
        "prep",
        [up[0]],
    )

    def stack(pieces, name):
        return call(stack_body, shape(len(pieces), bw, rows), pieces, (), name)

    f_near = exchange(stack([fr[k] for k in range(half)], "stack_f"), fwd_low, "mix_f")
    f_far = exchange(stack([fr[k] for k in range(half, nb)], "stack_f"), fwd_low, "mix_f")
    s_near = exchange(stack([sr[k] for k in range(half)], "stack_s"), fwd_low, "mix_s")
    s_far = exchange(stack([sr[k] for k in range(half, nb)], "stack_s"), fwd_low, "mix_s")

    f_last = fwd_low + 2 * (n_low - 1)
    a_last = adj_low + 2 * (n_low - 1)
    fo = call(
        functools.partial(forward_body, nb, f_last, fwd_loc),
        [shape(bw, rows)] * nb,
        [coef, blocks, w_own_t, *f_near, *f_far, *[fr[k] for k in range(nb)]],
        [pltpu.VMEM((nb, bw, rows), BF16)],
        "layer_f",
    )
    of = {k: send(fo[k], 0, k * low) for k in far_first[:-1]}
    of[0] = fo[0]

    v_near, v_far, d, act, gz, u = call(
        functools.partial(backward_body, nb, f_last, fwd_loc, adj_loc),
        [shape(half, bw, rows), shape(nb - half, bw, rows)] + [shape(nb, bw, rows)] * 4,
        [
            coef,
            blocks,
            w_own,
            w_own_t,
            *s_near,
            *s_far,
            *[sr[k] for k in range(nb)],
            *[ur[k] for k in range(nb)],
        ],
        [pltpu.VMEM((nb, bw, rows), F32)],
        "layer_b",
    )
    od = {}
    for v, k0, n in ((v_far, half, nb - half), (v_near, 0, half)):
        own, other = exchange(v, adj_low, "mix_d")
        outs = call(
            functools.partial(finish_body, k0, n, a_last),
            [shape(bw, rows)] * n,
            [coef, own, other, d],
            (),
            "finish_d",
        )
        for k in reversed(range(n)):
            od[k0 + k] = send(outs[k], 0, (k0 + k) * low) if k0 + k else outs[k]

    part = bw // low
    keep, give, gb = call(
        functools.partial(grads_body, nb),
        [shape(low // 2, part, bw, dtype=F32), shape(low // 2, part, bw), shape(rows, rows, dtype=F32)],
        [at, act, gz, d, u],
        [pltpu.VMEM((low, part, bw), F32)],
        "weight_grads",
    )
    for l in range(n_low):
        got = send(give, 0, 1 << l)
        if l < n_low - 1:
            n = low >> l + 2
            keep, give = call(
                functools.partial(halve_body, l + 1),
                [shape(n, part, bw, dtype=F32), shape(n, part, bw)],
                [at, keep, got],
                [pltpu.VMEM((2 * n, part, bw), F32)],
                "sum_w",
            )
    grad_w = call(add_body, shape(1, part, bw, dtype=F32), [keep, got], (), "sum_w", (), True)
    for l in range(levels):
        gb = call(add_body, shape(rows, rows, dtype=F32), [gb, send(gb, 0, 1 << l)], (), "sum_b", (), l == levels - 1)
    out_f = unpack([of[k] for k in range(nb)], "unpack_f")
    out_d = unpack([od[k] for k in range(nb)], "unpack_d")
    return out_f[None], out_d[None], grad_w, gb[None]


def solution(mesh):
    placed = (
        P("section", "seq", None),
        P("section", "seq", None),
        P("section", "seq", None),
        P("section", None, None),
        P("section", None, None, None),
        P("section", None, None),
    )
    return jax.shard_map(
        on_device,
        mesh=mesh,
        in_specs=placed,
        out_specs=(
            P("section", "seq", None),
            P("section", "seq", None),
            P("section", "seq", None),
            P("section", None, None),
        ),
        check_vma=False,
    )
```

```python
import functools

import jax
import jax.numpy as jnp
from jax import lax
from jax.experimental import pallas as pl
from jax.experimental.pallas import tpu as pltpu
from jax.sharding import PartitionSpec as P

F32 = jnp.float32
BF16 = jnp.bfloat16
LANES = 128
CH = 64
DECLARED = 8_000_000_000


def dot(a, b, ca, cb):
    return lax.dot_general(a, b, (((ca,), (cb,)), ((), ())), preferred_element_type=F32)


def near_memory(x):
    return pltpu.with_memory_space_constraint(x, pltpu.VMEM)


def call(body, outs, ins, scratch=(), name=None, deps=(), in_hbm=(), out_hbm=False, declared=0):
    n_in, n_dep = len(ins) + len(in_hbm), len(deps)

    def kernel(*refs):
        body(*refs[:n_in], *refs[n_in + n_dep :])

    specs = []
    args = []
    for a in ins:
        if a.dtype == jnp.int32:
            specs.append(pl.BlockSpec(memory_space=pltpu.SMEM))
            args.append(a)
        else:
            specs.append(pl.BlockSpec(memory_space=pltpu.VMEM))
            args.append(near_memory(a))
    for a in in_hbm:
        specs.append(pl.BlockSpec(memory_space=pltpu.HBM))
        args.append(pltpu.with_memory_space_constraint(a, pltpu.HBM))
    for a in deps:
        specs.append(pl.BlockSpec(memory_space=pl.ANY))
        args.append(a)
    shapes = jax.tree.map(lambda o: pltpu.VMEM(o.shape, o.dtype), outs)
    if out_hbm:
        shapes = [shapes[0], *[pltpu.HBM(o.shape, o.dtype) for o in outs[1:]]]
    return pl.pallas_call(
        kernel,
        out_shape=shapes,
        in_specs=specs,
        out_specs=jax.tree.map(lambda _: pl.BlockSpec(memory_space=pltpu.VMEM), outs),
        scratch_shapes=scratch,
        name=name,
        compiler_params=pltpu.CompilerParams(vmem_limit_bytes=6 << 20),
        cost_estimate=pl.CostEstimate(flops=declared, bytes_accessed=0, transcendentals=0),
    )(*args)


def shape(*dims, dtype=BF16):
    return jax.ShapeDtypeStruct(dims, dtype)


def pack_body(nb, at_ref, x_ref, *refs):
    outs, buf = refs[:nb], refs[nb]
    width = x_ref.shape[1]
    bw = width // nb
    for j in range(0, width, LANES):
        buf[j : j + LANES, :] = x_ref[:, j : j + LANES].T
    for k in range(nb):
        start = pl.multiple_of(jnp.bitwise_xor(at_ref[0], k) * bw, 16)
        outs[k][...] = buf[pl.ds(start, bw), :]


def open_body(nb, at_ref, x_hbm, *refs):
    n = (len(refs) - nb - 3) // 2
    hbm, outs, held = refs[:n], refs[n : n + nb], refs[n + nb : 2 * n + nb]
    x_ref, buf, sems = refs[2 * n + nb :]
    copies = [pltpu.make_async_copy(x_hbm, x_ref, sems.at[0])]
    copies += [pltpu.make_async_copy(a, b, sems.at[1 + i]) for i, (a, b) in enumerate(zip(hbm, held))]
    for c in copies:
        c.start()
    copies[0].wait()
    pack_body(nb, at_ref, x_ref, *outs, buf)
    for c in copies[1:]:
        c.wait()


def unpack_body(nb, at_ref, *refs):
    ins, token, out, buf = refs[:nb], refs[nb], refs[nb + 1], refs[nb + 2]
    width = out.shape[1]
    bw = width // nb
    for k in range(nb):
        start = pl.multiple_of(jnp.bitwise_xor(at_ref[0], k) * bw, 16)
        buf[pl.ds(start, bw), :] = ins[k][...]
    for j in range(0, width, LANES):
        out[:, j : j + LANES] = buf[j : j + LANES, :].T
    token[...] = jnp.zeros_like(token)


def prep_body(nb, n_low, at_ref, c_ref, w_ref, coef_ref, wo_ref, wt_ref, buf, table):
    levels, _, width = c_ref.shape
    bw = width // nb
    for b in range(nb):

        @pl.when(at_ref[0] == b)
        def _():
            cols = slice(b * bw, (b + 1) * bw)
            for l in range(levels):
                buf[4 * l : 4 * l + 4, :] = c_ref[l, :, cols]
            wt = w_ref[:, cols]
            wt_ref[...] = wt
            wo_ref[...] = wt.T

    row = 0
    for lower, upper, span in (
        ((0, 1, 3, 2), (3, 2, 0, 1), range(n_low, levels)),
        ((0, 1), (3, 2), range(n_low)),
        ((0, 2, 3, 1), (3, 1, 0, 2), range(n_low, levels)),
        ((0, 2), (3, 1), range(n_low)),
    ):
        for l in span:
            for a, b in zip(lower, upper):
                high = at_ref[1 + l] == 1
                i, j = 4 * l + b, 4 * l + a
                table[row : row + 1, :] = jnp.where(high, buf[i : i + 1, :], buf[j : j + 1, :])
                row += 1
    coef_ref[...] = table[...].T


def copy_body(*refs):
    n = len(refs) // 2
    for k in range(n):
        refs[n + k][...] = refs[k][...]


def mark_body(out_ref):
    out_ref[...] = jnp.zeros_like(out_ref)


def join_body(*refs):
    outs = refs[len(refs) // 3 * 2 :]
    for k, out in enumerate(outs):
        out[0] = refs[k][...]
        out[1] = refs[len(outs) + k][...]


def stack_body(*refs):
    out = refs[-1]
    for k, r in enumerate(refs[:-1]):
        out[k] = r[...]


def pair(coef_ref, first, s):
    return (coef_ref[s : s + CH, first : first + 1], coef_ref[s : s + CH, first + 1 : first + 2])


def combine_body(first, coef_ref, own_ref, other_ref, out_ref):
    for s in range(0, out_ref.shape[1], CH):
        c0, c1 = pair(coef_ref, first, s)
        for k in range(out_ref.shape[0]):
            own = own_ref[k, s : s + CH, :].astype(F32)
            other = other_ref[k, s : s + CH, :].astype(F32)
            out_ref[k, s : s + CH, :] = (c0 * own + c1 * other).astype(BF16)


def local_levels(vals, coef, first):
    vals = list(vals)
    nb = len(vals)
    for j in range(nb.bit_length() - 1):
        c = [coef[:, first + 4 * j + i : first + 4 * j + i + 1] for i in range(4)]
        for k in range(nb):
            if not k >> j & 1:
                m = k | 1 << j
                a, b = vals[k], vals[m]
                vals[k] = c[0] * a + c[1] * b
                vals[m] = c[2] * b + c[3] * a
    return vals


def finish_state(first, loc, coef_ref, chunks, u_ref):
    for s in range(0, u_ref.shape[1], CH):
        c0, c1 = pair(coef_ref, first, s)
        vals = []
        for own_ref, other_ref in chunks:
            for k in range(own_ref.shape[0]):
                vals.append(c0 * own_ref[k, s : s + CH, :].astype(F32) + c1 * other_ref[k, s : s + CH, :].astype(F32))
        vals = local_levels(vals, coef_ref[s : s + CH, :], loc)
        for k, v in enumerate(vals):
            u_ref[k, s : s + CH, :] = v.astype(BF16)


def mix_rows(u_ref, b_ref, ins, act_ref):
    for k, r in enumerate(ins):
        lanes = slice(k * LANES, (k + 1) * LANES)
        act_ref[:, lanes] = (r[...].astype(F32) + dot(u_ref[k], b_ref[...], 1, 1)).astype(BF16)


def forward_body(nb, first, loc, coef_ref, b_ref, wt_ref, own_ref, other_ref, *refs):
    ins, outs, u_ref, act_ref = refs[:nb], refs[nb : 2 * nb], refs[2 * nb], refs[2 * nb + 1]
    finish_state(first, loc, coef_ref, ((own_ref, other_ref),), u_ref)
    mix_rows(u_ref, b_ref, ins, act_ref)
    act = act_ref[...]
    pre = dot(wt_ref[...], act, 1, 0)
    out = (act.astype(F32) + pre * jax.nn.sigmoid(pre)).astype(BF16)
    for k in range(nb):
        outs[k][...] = out[:, k * LANES : (k + 1) * LANES]


def backward_body(nb, first, loc, adj, coef_ref, b_ref, w_ref, wt_ref, own_ref, other_ref, *refs):
    ins, ups = refs[:nb], refs[nb : 2 * nb]
    v0_ref, v1_ref, d_ref, act_ref, gz_ref, u_ref, v_ref, up_ref = refs[2 * nb :]
    finish_state(first, loc, coef_ref, ((own_ref, other_ref),), u_ref)
    mix_rows(u_ref, b_ref, ins, act_ref)
    for k in range(nb):
        up_ref[:, k * LANES : (k + 1) * LANES] = ups[k][...]
    pre = dot(wt_ref[...], act_ref[...], 1, 0)
    sig = jax.nn.sigmoid(pre)
    gz_ref[...] = (up_ref[...].astype(F32) * (sig * (1.0 + pre * (1.0 - sig)))).astype(BF16)
    back = dot(w_ref[...], gz_ref[...], 1, 0)
    d = (up_ref[...].astype(F32) + back).astype(BF16)
    for k in range(nb):
        d_ref[k] = d[:, k * LANES : (k + 1) * LANES]
        v_ref[k] = dot(d_ref[k], b_ref[...], 1, 0)
    half = nb // 2
    for s in range(0, d_ref.shape[1], CH):
        vals = local_levels([v_ref[k, s : s + CH, :] for k in range(nb)], coef_ref[s : s + CH, :], adj)
        for k in range(half):
            v0_ref[k, s : s + CH, :] = vals[k].astype(BF16)
            v1_ref[k, s : s + CH, :] = vals[half + k].astype(BF16)


def finish_body(k0, n, first, coef_ref, own_ref, other_ref, d_ref, *outs):
    for s in range(0, own_ref.shape[1], CH):
        c0, c1 = pair(coef_ref, first, s)
        for k in range(n):
            outs[k][s : s + CH, :] = (
                d_ref[k0 + k, s : s + CH, :].astype(F32)
                + c0 * own_ref[k, s : s + CH, :].astype(F32)
                + c1 * other_ref[k, s : s + CH, :].astype(F32)
            ).astype(BF16)


def halve(at_ref, l, src, keep_ref, send_ref):
    bit = at_ref[1 + l]
    for j in range(keep_ref.shape[0]):
        keep_ref[j] = src[2 * j + bit]
        send_ref[j] = src[2 * j + 1 - bit].astype(BF16)


def riders(n, rows, part, bw):
    places = []
    for i, r in enumerate(range(0, rows, part)):
        places.append((n + i // (bw // LANES), i % (bw // LANES) * LANES, r, min(part, rows - r)))
    return places, places[-1][0] + 1 - n


def grads_body(nb, act_ref, gz_ref, d_ref, u_ref, gw_ref, gb_ref):
    gw, gb = dot(act_ref[...], gz_ref[...], 1, 1), 0.0
    for k in range(nb):
        gb = gb + dot(d_ref[k], u_ref[k], 0, 0)
    gb_ref[...] = gb.astype(BF16)
    part = gw_ref.shape[1]
    for n in range(gw_ref.shape[0]):
        gw_ref[n] = gw[n * part : (n + 1) * part, :]


def ride(own, send_ref, n):
    for m, lane, r, count in riders(n, own.shape[0], send_ref.shape[1], send_ref.shape[2])[0]:
        send_ref[m, :count, lane : lane + LANES] = own[r : r + count, :].astype(BF16)


def first_half_body(at_ref, gw_ref, gb_ref, keep_ref, send_ref):
    halve(at_ref, 0, gw_ref, keep_ref, send_ref)
    ride(gb_ref, send_ref, keep_ref.shape[0])


def sum_riders(n, own_ref, other_ref, out_ref):
    rows, part, bw = own_ref.shape[0], other_ref.shape[1], other_ref.shape[2]
    for m, lane, r, count in riders(n, rows, part, bw)[0]:
        out_ref[r : r + count, :] = (
            own_ref[r : r + count, :].astype(F32) + other_ref[m, :count, lane : lane + LANES].astype(F32)
        ).astype(out_ref.dtype)


def halve_body(l, at_ref, own_ref, other_ref, gb_ref, keep_ref, send_ref, sum_ref, buf, wide):
    n = own_ref.shape[0]
    for j in range(n):
        buf[j] = own_ref[j] + other_ref[j].astype(F32)
    halve(at_ref, l, buf, keep_ref, send_ref)
    sum_riders(n, gb_ref, other_ref, wide)
    sum_ref[...] = wide[...].astype(BF16)
    ride(wide, send_ref, keep_ref.shape[0])


def last_body(own_ref, other_ref, gb_ref, token, out_ref, sum_ref):
    token[...] = jnp.zeros_like(token)
    n = own_ref.shape[0]
    for j in range(n):
        out_ref[j] = own_ref[j] + other_ref[j].astype(F32)
    sum_riders(n, gb_ref, other_ref, sum_ref)


def add_body(own_ref, other_ref, out_ref):
    out_ref[...] = (own_ref[...].astype(F32) + other_ref[...].astype(F32)).astype(out_ref.dtype)


class Chain:
    def __init__(self):
        self.last = []

    def __call__(self, *args, deps=(), **kwargs):
        outs = call(*args, deps=[*self.last, *deps], **kwargs)
        self.last = [jax.tree.leaves(outs)[0]]
        return outs


def on_device(prev_out, prev_grad, saved_in, seq_mix, coeffs, mixer):
    n_sec, n_seq = lax.axis_size("section"), lax.axis_size("seq")
    weights = mixer[0]
    width, bw = weights.shape
    nb = width // bw
    low = n_seq // nb
    levels = n_seq.bit_length() - 1
    n_low = low.bit_length() - 1
    n_top = levels - n_low
    q = lax.axis_index("seq").astype(jnp.int32)
    at = jnp.stack([q // low] + [jnp.bitwise_and(jnp.right_shift(q, l), 1) for l in range(levels)])
    rows = prev_out.shape[1]
    half = nb // 2
    fwd_loc, fwd_low = 0, 4 * n_top
    adj_loc = fwd_low + 2 * n_low
    adj_low = adj_loc + 4 * n_top
    n_coef = adj_low + 2 * n_low

    def send(x, shift, flip, name="p"):
        with jax.named_scope(name):
            return send_(x, shift, flip)

    def send_(x, shift, flip):
        pairs = [
            (s * n_seq + i, (s + shift) % n_sec * n_seq + (i ^ flip)) for s in range(n_sec) for i in range(n_seq)
        ]
        return lax.ppermute(x, ("section", "seq"), pairs)

    run = Chain()

    def pack(x, name, deps=()):
        return run(
            functools.partial(pack_body, nb),
            [shape(bw, rows)] * nb,
            [at, x],
            [pltpu.VMEM((width, rows), BF16)],
            name,
            deps=deps,
        )

    token = shape(8, LANES, dtype=F32)

    def unpack(pieces, name):
        return run(
            functools.partial(unpack_body, nb),
            [token, shape(rows, width)],
            [at, *[pieces[k] for k in range(nb)]],
            [pltpu.VMEM((width, rows), BF16)],
            name,
            out_hbm=True,
        )[1]

    def release(pieces, name, deps=()):
        return run(copy_body, [shape(*p.shape) for p in pieces], pieces, (), name, deps=deps)

    def stack(pieces, name, deps=()):
        return run(stack_body, shape(nb, bw, rows), [pieces[k] for k in range(nb)], (), name, deps=deps)

    def cross(u, flip, name):
        if name in ():
            return send(u, 0, flip, name), u
        mark = call(mark_body, shape(8, LANES, dtype=F32), [], (), "mark", [u], declared=DECLARED)
        return send(u, 0, flip, name), mark

    def open_step(u, name):
        return u, *cross(u, 1, f"{name}_level0")

    def more_steps(opened, first, name):
        u, other, mark = opened
        for l in range(1, n_low):
            u = run(
                functools.partial(combine_body, first + 2 * (l - 1)),
                shape(*u.shape),
                [coef, u, other],
                (),
                f"mix_{name}",
                deps=[mark],
            )
            other, mark = cross(u, 1 << l, f"{name}_level{l}")
        return u, other, mark

    far = range(half, nb)
    far_first = [*reversed(far), *reversed(range(1, half))]

    def spread(pieces, shift, ks, name):
        return {k: send(pieces[k], shift, k * low, f"{name}{k}") for k in ks}

    held = [saved_in[0], prev_grad[0], coeffs[0], weights.T, seq_mix[0]]
    *fp, saved, upstream, factors, w_t, blocks = run(
        functools.partial(open_body, nb),
        [shape(bw, rows)] * nb + [shape(*a.shape, dtype=a.dtype) for a in held],
        [at],
        [
            pltpu.VMEM((rows, width), BF16),
            pltpu.VMEM((width, rows), BF16),
            pltpu.SemaphoreType.DMA((1 + len(held),)),
        ],
        "pack_f",
        in_hbm=[prev_out[0], *held],
    )
    fr = spread(fp, 1, [*range(1, half), 0, *far], "in_f")
    sp = pack(saved, "pack_s", [fr[k] for k in range(half)])
    sr = {0: sp[0], **spread(sp, 0, range(1, nb), "in_s")}
    coef, w_own, w_own_t = run(
        functools.partial(prep_body, nb, n_low),
        [shape(bw, n_coef, dtype=F32), shape(bw, bw), shape(bw, bw)],
        [at, factors, w_t],
        [pltpu.VMEM((4 * levels, bw), F32), pltpu.VMEM((n_coef, bw), F32)],
        "prep",
    )
    f_open = open_step(stack(fr, "stack_f", [sr[k] for k in range(1, half)]), "f")
    f_all = more_steps(f_open, fwd_low, "f")
    up = pack(upstream, "pack_u")
    ur = spread(up, -1, far, "in_u")
    s_open = open_step(stack(sr, "stack_s"), "s")
    s_all = more_steps(s_open, fwd_low, "s")
    u_near = release(up[:half], "release_u")
    ur.update(spread(u_near, -1, range(half), "in_u"))

    f_last = fwd_low + 2 * (n_low - 1)
    a_last = adj_low + 2 * (n_low - 1)
    fo = run(
        functools.partial(forward_body, nb, f_last, fwd_loc),
        [shape(bw, rows)] * nb,
        [coef, blocks, w_own_t, *f_all[:2], *[fr[k] for k in range(nb)]],
        [pltpu.VMEM((nb, bw, rows), BF16), pltpu.VMEM((bw, nb * rows), BF16)],
        "layer_f",
        deps=[f_all[2]],
    )
    of = {0: fo[0], **spread(fo, 0, far_first, "out_f")}

    v_near, v_far, d, act, gz, u = run(
        functools.partial(backward_body, nb, f_last, fwd_loc, adj_loc),
        [shape(half, bw, rows), shape(nb - half, bw, rows), shape(nb, bw, rows)]
        + [shape(bw, nb * rows)] * 2
        + [shape(nb, bw, rows)],
        [
            coef,
            blocks,
            w_own,
            w_own_t,
            *s_all[:2],
            *[sr[k] for k in range(nb)],
            *[ur[k] for k in range(nb)],
        ],
        [pltpu.VMEM((nb, bw, rows), F32), pltpu.VMEM((bw, nb * rows), BF16)],
        "layer_b",
        deps=[s_all[2]],
    )
    far_open, near_open = open_step(v_far, "d_far"), open_step(v_near, "d_near")
    part = bw // low
    gb_slabs = riders(0, rows, part, bw)[1]
    gw, gb = run(
        functools.partial(grads_body, nb),
        [shape(low, part, bw, dtype=F32), shape(rows, rows)],
        [act, gz, d, u],
        (),
        "weight_grads",
    )
    d_far = more_steps(far_open, adj_low, "d_far")
    d_near = more_steps(near_open, adj_low, "d_near")
    out_f = unpack(of, "unpack_f")
    od = {}

    def finish(opened, k0, n):
        own, other, mark = opened
        outs = run(
            functools.partial(finish_body, k0, n, a_last),
            [shape(bw, rows)] * n,
            [coef, own, other, d],
            (),
            "finish_d",
            deps=[mark],
        )
        for k in reversed(range(n)):
            od[k0 + k] = send(outs[k], 0, (k0 + k) * low, f"out_d{k0 + k}") if k0 + k else outs[k]

    def sum_b(gb, l):
        got, mark = cross(gb, 1 << l, f"sum_b{l}")
        return run(add_body, shape(rows, rows), [gb, got], (), "sum_b", deps=[mark])

    gb = sum_b(gb, n_low)
    finish(d_far, half, nb - half)
    for l in range(n_low + 1, levels):
        gb = sum_b(gb, l)
    keep, give = run(
        first_half_body,
        [shape(low // 2, part, bw, dtype=F32), shape(low // 2 + gb_slabs, part, bw)],
        [at, gw, gb],
        (),
        "sum_w",
    )
    got, mark = cross(give, 1, "sum_w0")
    finish(d_near, 0, half)
    for l in range(n_low - 1):
        m = low >> l + 2
        keep, give, gb = run(
            functools.partial(halve_body, l + 1),
            [shape(m, part, bw, dtype=F32), shape(m + gb_slabs, part, bw), shape(rows, rows)],
            [at, keep, got, gb],
            [pltpu.VMEM((2 * m, part, bw), F32), pltpu.VMEM((rows, rows), F32)],
            "sum_w",
            deps=[mark],
        )
        got, mark = cross(give, 2 << l, f"sum_w{l + 1}")
    _, grad_w, grad_b = run(
        last_body,
        [token, shape(1, part, bw, dtype=F32), shape(rows, rows, dtype=F32)],
        [keep, got, gb],
        (),
        "sum_w",
        deps=[mark],
        out_hbm=True,
    )
    out_d = unpack(od, "unpack_d")
    return out_f[None], out_d[None], grad_w, grad_b[None]


def solution(mesh):
    placed = (
        P("section", "seq", None),
        P("section", "seq", None),
        P("section", "seq", None),
        P("section", None, None),
        P("section", None, None, None),
        P("section", None, None),
    )
    return jax.shard_map(
        on_device,
        mesh=mesh,
        in_specs=placed,
        out_specs=(
            P("section", "seq", None),
            P("section", "seq", None),
            P("section", "seq", None),
            P("section", None, None),
        ),
        check_vma=False,
    )
```

```python
import functools

import jax
import jax.numpy as jnp
from jax import lax
from jax.experimental import pallas as pl
from jax.experimental.pallas import tpu as pltpu
from jax.sharding import PartitionSpec as P

F32 = jnp.float32
BF16 = jnp.bfloat16
LANES = 128
CH = 64
DECLARED = 8_000_000_000
STEP = 200_000_000


def dot(a, b, ca, cb):
    return lax.dot_general(a, b, (((ca,), (cb,)), ((), ())), preferred_element_type=F32)


def near_memory(x):
    return pltpu.with_memory_space_constraint(x, pltpu.VMEM)


def call(body, outs, ins, scratch=(), name=None, deps=(), in_hbm=(), out_hbm=False, declared=0):
    n_in, n_dep = len(ins) + len(in_hbm), len(deps)

    def kernel(*refs):
        body(*refs[:n_in], *refs[n_in + n_dep :])

    specs = []
    args = []
    for a in ins:
        if a.dtype == jnp.int32:
            specs.append(pl.BlockSpec(memory_space=pltpu.SMEM))
            args.append(a)
        else:
            specs.append(pl.BlockSpec(memory_space=pltpu.VMEM))
            args.append(near_memory(a))
    for a in in_hbm:
        specs.append(pl.BlockSpec(memory_space=pltpu.HBM))
        args.append(pltpu.with_memory_space_constraint(a, pltpu.HBM))
    for a in deps:
        specs.append(pl.BlockSpec(memory_space=pl.ANY))
        args.append(a)
    shapes = jax.tree.map(lambda o: pltpu.VMEM(o.shape, o.dtype), outs)
    if out_hbm:
        shapes = [shapes[0], *[pltpu.HBM(o.shape, o.dtype) for o in outs[1:]]]
    return pl.pallas_call(
        kernel,
        out_shape=shapes,
        in_specs=specs,
        out_specs=jax.tree.map(lambda _: pl.BlockSpec(memory_space=pltpu.VMEM), outs),
        scratch_shapes=scratch,
        name=name,
        compiler_params=pltpu.CompilerParams(vmem_limit_bytes=6 << 20),
        cost_estimate=pl.CostEstimate(flops=declared, bytes_accessed=0, transcendentals=0),
    )(*args)


def shape(*dims, dtype=BF16):
    return jax.ShapeDtypeStruct(dims, dtype)


def pack_body(nb, at_ref, x_ref, *refs):
    outs, buf = refs[:nb], refs[nb]
    width = x_ref.shape[1]
    bw = width // nb
    for j in range(0, width, LANES):
        buf[j : j + LANES, :] = x_ref[:, j : j + LANES].T
    for k in range(nb):
        start = pl.multiple_of(jnp.bitwise_xor(at_ref[0], k) * bw, 16)
        outs[k][...] = buf[pl.ds(start, bw), :]


def unpack_last_body(nb, at_ref, *refs):
    ins, own_ref = refs[:nb], refs[nb]
    token, out, sum_ref, buf = refs[nb + 1 :]
    add_last_body(own_ref, ins[nb // 2], token, sum_ref)
    unpack_body(nb, at_ref, *ins, token, out, buf)


def open_body(nb, at_ref, x_hbm, *refs):
    n = (len(refs) - nb - 3) // 2
    hbm, outs, held = refs[:n], refs[n : n + nb], refs[n + nb : 2 * n + nb]
    x_ref, buf, sems = refs[2 * n + nb :]
    copies = [pltpu.make_async_copy(x_hbm, x_ref, sems.at[0])]
    copies += [pltpu.make_async_copy(a, b, sems.at[1 + i]) for i, (a, b) in enumerate(zip(hbm, held))]
    for c in copies:
        c.start()
    copies[0].wait()
    pack_body(nb, at_ref, x_ref, *outs, buf)
    for c in copies[1:]:
        c.wait()


def unpack_body(nb, at_ref, *refs):
    ins, token, out, buf = refs[:nb], refs[nb], refs[nb + 1], refs[nb + 2]
    width = out.shape[1]
    bw = width // nb
    for k in range(nb):
        start = pl.multiple_of(jnp.bitwise_xor(at_ref[0], k) * bw, 16)
        buf[pl.ds(start, bw), :] = ins[k][0:bw, :]
    for j in range(0, width, LANES):
        out[:, j : j + LANES] = buf[j : j + LANES, :].T
    token[...] = jnp.zeros_like(token)


def prep_body(nb, n_low, at_ref, c_ref, w_ref, coef_ref, wo_ref, wt_ref, buf, table):
    levels, _, width = c_ref.shape
    bw = width // nb
    for b in range(nb):

        @pl.when(at_ref[0] == b)
        def _():
            cols = slice(b * bw, (b + 1) * bw)
            for l in range(levels):
                buf[4 * l : 4 * l + 4, :] = c_ref[l, :, cols]
            wt = w_ref[:, cols]
            wt_ref[...] = wt
            wo_ref[...] = wt.T

    row = 0
    for lower, upper, span in (
        ((0, 1, 3, 2), (3, 2, 0, 1), range(n_low, levels)),
        ((0, 1), (3, 2), range(n_low)),
        ((0, 2, 3, 1), (3, 1, 0, 2), range(n_low, levels)),
        ((0, 2), (3, 1), range(n_low)),
    ):
        for l in span:
            for a, b in zip(lower, upper):
                high = at_ref[1 + l] == 1
                i, j = 4 * l + b, 4 * l + a
                table[row : row + 1, :] = jnp.where(high, buf[i : i + 1, :], buf[j : j + 1, :])
                row += 1
    coef_ref[...] = table[...].T


def copy_body(*refs):
    n = len(refs) // 2
    for k in range(n):
        refs[n + k][...] = refs[k][...]


def mark_body(out_ref):
    out_ref[...] = jnp.zeros_like(out_ref)


def stack_body(*refs):
    out = refs[-1]
    for k, r in enumerate(refs[:-1]):
        out[k] = r[...]


def pair(coef_ref, first, s):
    return (coef_ref[s : s + CH, first : first + 1], coef_ref[s : s + CH, first + 1 : first + 2])


def combine_body(first, coef_ref, own_ref, other_ref, out_ref):
    for s in range(0, out_ref.shape[1], CH):
        c0, c1 = pair(coef_ref, first, s)
        for k in range(out_ref.shape[0]):
            own = own_ref[k, s : s + CH, :].astype(F32)
            other = other_ref[k, s : s + CH, :].astype(F32)
            out_ref[k, s : s + CH, :] = (c0 * own + c1 * other).astype(BF16)


def local_levels(vals, coef, first):
    vals = list(vals)
    nb = len(vals)
    for j in range(nb.bit_length() - 1):
        c = [coef[:, first + 4 * j + i : first + 4 * j + i + 1] for i in range(4)]
        for k in range(nb):
            if not k >> j & 1:
                m = k | 1 << j
                a, b = vals[k], vals[m]
                vals[k] = c[0] * a + c[1] * b
                vals[m] = c[2] * b + c[3] * a
    return vals


def finish_state(first, loc, coef_ref, chunks, u_ref):
    for s in range(0, u_ref.shape[1], CH):
        c0, c1 = pair(coef_ref, first, s)
        vals = []
        for own_ref, other_ref in chunks:
            for k in range(own_ref.shape[0]):
                vals.append(c0 * own_ref[k, s : s + CH, :].astype(F32) + c1 * other_ref[k, s : s + CH, :].astype(F32))
        vals = local_levels(vals, coef_ref[s : s + CH, :], loc)
        for k, v in enumerate(vals):
            u_ref[k, s : s + CH, :] = v.astype(BF16)


def mix_rows(u_ref, b_ref, ins, act_ref):
    for k, r in enumerate(ins):
        lanes = slice(k * LANES, (k + 1) * LANES)
        act_ref[:, lanes] = (r[...].astype(F32) + dot(u_ref[k], b_ref[...], 1, 1)).astype(BF16)


def forward_body(nb, first, loc, coef_ref, b_ref, wt_ref, own0, other0, own1, other1, *refs):
    ins, outs, u_ref, act_ref = refs[:nb], refs[nb : 2 * nb], refs[2 * nb], refs[2 * nb + 1]
    finish_state(first, loc, coef_ref, ((own0, other0), (own1, other1)), u_ref)
    mix_rows(u_ref, b_ref, ins, act_ref)
    act = act_ref[...]
    pre = dot(wt_ref[...], act, 1, 0)
    out = (act.astype(F32) + pre * jax.nn.sigmoid(pre)).astype(BF16)
    for k in range(nb):
        outs[k][...] = out[:, k * LANES : (k + 1) * LANES]


def backward_body(nb, first, loc, adj, coef_ref, b_ref, w_ref, wt_ref, own_ref, other_ref, *refs):
    ins, ups = refs[:nb], refs[nb : 2 * nb]
    v0_ref, v1_ref, d_ref, act_ref, gz_ref, u_ref, v_ref, up_ref = refs[2 * nb :]
    finish_state(first, loc, coef_ref, ((own_ref, other_ref),), u_ref)
    mix_rows(u_ref, b_ref, ins, act_ref)
    for k in range(nb):
        up_ref[:, k * LANES : (k + 1) * LANES] = ups[k][...]
    pre = dot(wt_ref[...], act_ref[...], 1, 0)
    sig = jax.nn.sigmoid(pre)
    gz_ref[...] = (up_ref[...].astype(F32) * (sig * (1.0 + pre * (1.0 - sig)))).astype(BF16)
    back = dot(w_ref[...], gz_ref[...], 1, 0)
    d = (up_ref[...].astype(F32) + back).astype(BF16)
    for k in range(nb):
        d_ref[k] = d[:, k * LANES : (k + 1) * LANES]
        v_ref[k] = dot(d_ref[k], b_ref[...], 1, 0)
    half = nb // 2
    for s in range(0, d_ref.shape[1], CH):
        vals = local_levels([v_ref[k, s : s + CH, :] for k in range(nb)], coef_ref[s : s + CH, :], adj)
        for k in range(half):
            v0_ref[k, s : s + CH, :] = vals[k].astype(BF16)
            v1_ref[k, s : s + CH, :] = vals[half + k].astype(BF16)


def finish_body(k0, n, first, coef_ref, own_ref, other_ref, d_ref, *outs):
    for s in range(0, own_ref.shape[1], CH):
        c0, c1 = pair(coef_ref, first, s)
        for k in range(n):
            outs[k][s : s + CH, :] = (
                d_ref[k0 + k, s : s + CH, :].astype(F32)
                + c0 * own_ref[k, s : s + CH, :].astype(F32)
                + c1 * other_ref[k, s : s + CH, :].astype(F32)
            ).astype(BF16)


def halve(at_ref, l, src, keep_ref, send_ref):
    bit = at_ref[1 + l]
    for j in range(keep_ref.shape[0]):
        keep_ref[j] = src[2 * j + bit]
        send_ref[j] = src[2 * j + 1 - bit].astype(BF16)


def grads_body(nb, act_ref, gz_ref, d_ref, u_ref, gw_ref, gb_ref):
    gw, gb = dot(act_ref[...], gz_ref[...], 1, 1), 0.0
    for k in range(nb):
        gb = gb + dot(d_ref[k], u_ref[k], 0, 0)
    gb_ref[...] = gb.astype(BF16)
    part = gw_ref.shape[1]
    for m in range(gw_ref.shape[0]):
        gw_ref[m] = gw[m * part : (m + 1) * part, :]


def join_gb_body(v_ref, gb_ref, near_ref):
    n, bw, _ = v_ref.shape
    for k in range(n):
        near_ref[k * bw : (k + 1) * bw, :] = v_ref[k]
    near_ref[n * bw :, :] = gb_ref[...]


def first_half_body(at_ref, gw_ref, keep_ref, send_ref):
    halve(at_ref, 0, gw_ref, keep_ref, send_ref)


def halve_body(l, at_ref, own_ref, other_ref, keep_ref, send_ref, buf):
    for j in range(own_ref.shape[0]):
        buf[j] = own_ref[j] + other_ref[j].astype(F32)
    halve(at_ref, l, buf, keep_ref, send_ref)


def last_body(own_ref, other_ref, token, out_ref):
    token[...] = jnp.zeros_like(token)
    out_ref[...] = own_ref[...] + other_ref[...].astype(F32)


def combine_riding_body(first, n, coef_ref, own_ref, other_ref, out_ref):
    bw = coef_ref.shape[0]
    for s in range(0, bw, CH):
        c0, c1 = pair(coef_ref, first, s)
        for k in range(n):
            r = slice(k * bw + s, k * bw + s + CH)
            out_ref[r, :] = (c0 * own_ref[r, :].astype(F32) + c1 * other_ref[r, :].astype(F32)).astype(BF16)
    r = slice(n * bw, out_ref.shape[0])
    out_ref[r, :] = (own_ref[r, :].astype(F32) + other_ref[r, :].astype(F32)).astype(BF16)


def finish_riding_body(n, first, coef_ref, own_ref, other_ref, d_ref, *outs):
    bw = coef_ref.shape[0]
    for s in range(0, bw, CH):
        c0, c1 = pair(coef_ref, first, s)
        for k in range(n):
            r = slice(k * bw + s, k * bw + s + CH)
            outs[k][s : s + CH, :] = (
                d_ref[k, s : s + CH, :].astype(F32)
                + c0 * own_ref[r, :].astype(F32)
                + c1 * other_ref[r, :].astype(F32)
            ).astype(BF16)
    r = slice(n * bw, own_ref.shape[0])
    outs[n][...] = (own_ref[r, :].astype(F32) + other_ref[r, :].astype(F32)).astype(BF16)


def join_sum_body(piece_ref, own_ref, other_ref, out_ref):
    n = piece_ref.shape[0]
    out_ref[0:n, :] = piece_ref[...]
    out_ref[n:, :] = (own_ref[...].astype(F32) + other_ref[...].astype(F32)).astype(BF16)


def add_last_body(own_ref, other_ref, token, out_ref):
    token[...] = jnp.zeros_like(token)
    r = slice(own_ref.shape[0] - out_ref.shape[0], own_ref.shape[0])
    out_ref[...] = own_ref[r, :].astype(F32) + other_ref[r, :].astype(F32)


class Chain:
    def __init__(self):
        self.last = []

    def __call__(self, *args, deps=(), **kwargs):
        outs = call(*args, deps=[*self.last, *deps], declared=STEP, **kwargs)
        self.last = [jax.tree.leaves(outs)[0]]
        return outs


def on_device(prev_out, prev_grad, saved_in, seq_mix, coeffs, mixer):
    n_sec, n_seq = lax.axis_size("section"), lax.axis_size("seq")
    weights = mixer[0]
    width, bw = weights.shape
    nb = width // bw
    low = n_seq // nb
    levels = n_seq.bit_length() - 1
    n_low = low.bit_length() - 1
    n_top = levels - n_low
    q = lax.axis_index("seq").astype(jnp.int32)
    at = jnp.stack([q // low] + [jnp.bitwise_and(jnp.right_shift(q, l), 1) for l in range(levels)])
    rows = prev_out.shape[1]
    half = nb // 2
    fwd_loc, fwd_low = 0, 4 * n_top
    adj_loc = fwd_low + 2 * n_low
    adj_low = adj_loc + 4 * n_top
    n_coef = adj_low + 2 * n_low

    def send(x, shift, flip, name="p"):
        with jax.named_scope(name):
            return send_(x, shift, flip)

    def send_(x, shift, flip):
        pairs = [
            (s * n_seq + i, (s + shift) % n_sec * n_seq + (i ^ flip)) for s in range(n_sec) for i in range(n_seq)
        ]
        return lax.ppermute(x, ("section", "seq"), pairs)

    run = Chain()

    def pack(x, name, deps=()):
        return run(
            functools.partial(pack_body, nb),
            [shape(bw, rows)] * nb,
            [at, x],
            [pltpu.VMEM((width, rows), BF16)],
            name,
            deps=deps,
        )

    token = shape(8, LANES, dtype=F32)

    def unpack(pieces, name):
        return run(
            functools.partial(unpack_body, nb),
            [token, shape(rows, width)],
            [at, *[pieces[k] for k in range(nb)]],
            [pltpu.VMEM((width, rows), BF16)],
            name,
            out_hbm=True,
        )[1]

    def release(pieces, name, deps=()):
        return run(copy_body, [shape(*p.shape) for p in pieces], pieces, (), name, deps=deps)

    def stack(pieces, name, deps=()):
        return run(stack_body, shape(len(pieces), bw, rows), pieces, (), name, deps=deps)

    def beside(u, work):
        return call(mark_body, shape(8, LANES, dtype=F32), [], (), "mark", [u], declared=work)

    def cross(u, flip, name):
        if name in ("fn_level1", "ff_level1", "s_level1", "d_far_level1", "d_near_level1"):
            return send(u, 0, flip, name), u
        mark = call(mark_body, shape(8, LANES, dtype=F32), [], (), "mark", [u], declared=11500 * u.size * 2)
        return send(u, 0, flip, name), mark

    def open_step(u, name):
        return u, *cross(u, 1, f"{name}_level0")

    def more_steps(opened, first, name, deps=()):
        u, other, mark = opened
        for l in range(1, n_low):
            u = run(
                functools.partial(combine_body, first + 2 * (l - 1)),
                shape(*u.shape),
                [coef, u, other],
                (),
                f"mix_{name}",
                deps=[mark, *deps],
            )
            other, mark = cross(u, 1 << l, f"{name}_level{l}")
        return u, other, mark

    far = range(half, nb)
    far_first = [*reversed(far), *reversed(range(1, half))]

    def spread(pieces, shift, ks, name):
        return {k: send(pieces[k], shift, k * low, f"{name}{k}") for k in ks}

    held = [prev_grad[0], prev_out[0], coeffs[0], weights.T, seq_mix[0]]
    *sp, upstream, incoming, factors, w_t, blocks = run(
        functools.partial(open_body, nb),
        [shape(bw, rows)] * nb + [shape(*a.shape, dtype=a.dtype) for a in held],
        [at],
        [
            pltpu.VMEM((rows, width), BF16),
            pltpu.VMEM((width, rows), BF16),
            pltpu.SemaphoreType.DMA((1 + len(held),)),
        ],
        "pack_s",
        in_hbm=[saved_in[0], *held],
    )
    sr = {0: sp[0], **spread(sp, 0, range(1, nb), "in_s")}
    up = pack(upstream, "pack_u")
    ur = spread(up, -1, [*reversed(range(half)), *far[:-1]], "in_u")
    coef, w_own, w_own_t = run(
        functools.partial(prep_body, nb, n_low),
        [shape(bw, n_coef, dtype=F32), shape(bw, bw), shape(bw, bw)],
        [at, factors, w_t],
        [pltpu.VMEM((4 * levels, bw), F32), pltpu.VMEM((n_coef, bw), F32)],
        "prep",
        deps=[sr[1]],
    )
    s_open = open_step(stack([sr[k] for k in range(nb)], "stack_s"), "s")
    fp = pack(incoming, "pack_f")
    s_all = more_steps(s_open, fwd_low, "s", [ur[k] for k in range(half)])
    fr = spread(fp, 1, reversed(range(half)), "in_f")
    ur[nb - 1] = spread({nb - 1: release(up[nb - 1 :], "release_u", [ur[half]])[0]}, -1, [nb - 1], "in_u")[nb - 1]
    f_far = release(fp[half:], "release_f", [ur[half]])
    fr.update(spread(dict(zip(far, f_far)), 1, far, "in_f"))
    near_open = open_step(stack([fr[k] for k in range(half)], "stack_fn"), "fn")
    fn = more_steps(near_open, fwd_low, "fn")

    f_last = fwd_low + 2 * (n_low - 1)
    a_last = adj_low + 2 * (n_low - 1)
    v_near, v_far, d, act, gz, u = run(
        functools.partial(backward_body, nb, f_last, fwd_loc, adj_loc),
        [shape(half, bw, rows), shape(nb - half, bw, rows), shape(nb, bw, rows)]
        + [shape(bw, nb * rows)] * 2
        + [shape(nb, bw, rows)],
        [
            coef,
            blocks,
            w_own,
            w_own_t,
            *s_all[:2],
            *[sr[k] for k in range(nb)],
            *[ur[k] for k in range(nb)],
        ],
        [pltpu.VMEM((nb, bw, rows), F32), pltpu.VMEM((bw, nb * rows), BF16)],
        "layer_b",
        deps=[s_all[2]],
    )
    far_open = open_step(v_far, "d_far")
    part = bw // low
    gw, gb = run(
        functools.partial(grads_body, nb),
        [shape(low, part, bw, dtype=F32), shape(rows, rows)],
        [act, gz, d, u],
        (),
        "weight_grads",
    )
    near = run(join_gb_body, shape(half * bw + rows, rows), [v_near, gb], (), "join_near")
    own, other, mark_n = open_step(near, "d_near")
    keep, give = run(
        first_half_body,
        [shape(low // 2, part, bw, dtype=F32), shape(low // 2, part, bw)],
        [at, gw],
        (),
        "sum_w",
    )
    got, mark = cross(give, 1, "sum_w0")
    d_far = more_steps(far_open, adj_low, "d_far")
    for l in range(1, n_low):
        own = run(
            functools.partial(combine_riding_body, adj_low + 2 * (l - 1), half),
            shape(*near.shape),
            [coef, own, other],
            (),
            "mix_d_near",
            deps=[mark_n],
        )
        other, mark_n = cross(own, 1 << l, f"d_near_level{l}")
    d_near = own, other, mark_n
    ff = more_steps(open_step(stack([fr[k] for k in far], "stack_ff"), "ff"), fwd_low, "ff", [fn[1]])
    own, other, ready = d_far
    outs = run(
        functools.partial(finish_body, half, nb - half, a_last),
        [shape(bw, rows)] * (nb - half),
        [coef, own, other, d],
        (),
        "finish_far",
        deps=[ready],
    )
    od = spread(dict(zip(far, outs)), 0, reversed(far), "out_d")
    for l in range(n_low - 1):
        m = low >> l + 2
        keep, give = run(
            functools.partial(halve_body, l + 1),
            [shape(m, part, bw, dtype=F32), shape(m, part, bw)],
            [at, keep, got],
            [pltpu.VMEM((2 * m, part, bw), F32)],
            "sum_w",
            deps=[mark],
        )
        got, mark = cross(give, 2 << l, f"sum_w{l + 1}")
    own, other, ready = d_near
    outs = run(
        functools.partial(finish_riding_body, half, a_last),
        [shape(bw, rows)] * half + [shape(rows, rows)],
        [coef, own, other, d],
        (),
        "finish_near",
        deps=[ready],
    )
    *outs, gb = outs
    od[0] = outs[0]
    od.update(spread(dict(enumerate(outs)), 0, range(1, half), "out_d"))
    got_b, mark_b = cross(gb, low, "sum_b0")
    fo = run(
        functools.partial(forward_body, nb, f_last, fwd_loc),
        [shape(bw, rows)] * nb,
        [coef, blocks, w_own_t, *fn[:2], *ff[:2], *[fr[k] for k in range(nb)]],
        [pltpu.VMEM((nb, bw, rows), BF16), pltpu.VMEM((bw, nb * rows), BF16)],
        "layer_f",
        deps=[fn[2], ff[2]],
    )
    of = {0: fo[0], **spread(fo, 0, [k for k in far_first if k != half], "out_f")}
    last_piece = run(
        join_sum_body,
        shape(bw + rows, rows),
        [fo[half], gb, got_b],
        (),
        "join_f",
        deps=[mark_b, od[nb - 1]],
    )
    of[half] = send(last_piece, 0, half * low, f"out_f{half}")
    out_d = unpack(od, "unpack_d")
    _, grad_w = run(
        last_body,
        [token, shape(1, part, bw, dtype=F32)],
        [keep, got],
        (),
        "sum_w",
        deps=[mark],
        out_hbm=True,
    )
    _, out_f, grad_b = run(
        functools.partial(unpack_last_body, nb),
        [token, shape(rows, width), shape(rows, rows, dtype=F32)],
        [at, *[of[k] for k in range(nb)], last_piece],
        [pltpu.VMEM((width, rows), BF16)],
        "unpack_f",
        out_hbm=True,
    )
    return out_f[None], out_d[None], grad_w, grad_b[None]


def solution(mesh):
    placed = (
        P("section", "seq", None),
        P("section", "seq", None),
        P("section", "seq", None),
        P("section", None, None),
        P("section", None, None, None),
        P("section", None, None),
    )
    return jax.shard_map(
        on_device,
        mesh=mesh,
        in_specs=placed,
        out_specs=(
            P("section", "seq", None),
            P("section", "seq", None),
            P("section", "seq", None),
            P("section", None, None),
        ),
        check_vma=False,
    )
```

```python
import functools

import jax
import jax.numpy as jnp
from jax import lax
from jax.experimental import pallas as pl
from jax.experimental.pallas import tpu as pltpu
from jax.sharding import PartitionSpec as P

F32 = jnp.float32
BF16 = jnp.bfloat16
LANES = 128
CH = 64
DECLARED = 8_000_000_000
STEP = 200_000_000


def dot(a, b, ca, cb):
    return lax.dot_general(a, b, (((ca,), (cb,)), ((), ())), preferred_element_type=F32)


def near_memory(x):
    return pltpu.with_memory_space_constraint(x, pltpu.VMEM)


def call(body, outs, ins, scratch=(), name=None, deps=(), in_hbm=(), out_hbm=False, declared=0):
    n_in, n_dep = len(ins) + len(in_hbm), len(deps)

    def kernel(*refs):
        body(*refs[:n_in], *refs[n_in + n_dep :])

    specs = []
    args = []
    for a in ins:
        if a.dtype == jnp.int32:
            specs.append(pl.BlockSpec(memory_space=pltpu.SMEM))
            args.append(a)
        else:
            specs.append(pl.BlockSpec(memory_space=pltpu.VMEM))
            args.append(near_memory(a))
    for a in in_hbm:
        specs.append(pl.BlockSpec(memory_space=pltpu.HBM))
        args.append(pltpu.with_memory_space_constraint(a, pltpu.HBM))
    for a in deps:
        specs.append(pl.BlockSpec(memory_space=pl.ANY))
        args.append(a)
    shapes = jax.tree.map(lambda o: pltpu.VMEM(o.shape, o.dtype), outs)
    if out_hbm:
        shapes = [shapes[0], *[pltpu.HBM(o.shape, o.dtype) for o in outs[1:]]]
    return pl.pallas_call(
        kernel,
        out_shape=shapes,
        in_specs=specs,
        out_specs=jax.tree.map(lambda _: pl.BlockSpec(memory_space=pltpu.VMEM), outs),
        scratch_shapes=scratch,
        name=name,
        compiler_params=pltpu.CompilerParams(vmem_limit_bytes=6 << 20),
        cost_estimate=pl.CostEstimate(flops=declared, bytes_accessed=0, transcendentals=0),
    )(*args)


def shape(*dims, dtype=BF16):
    return jax.ShapeDtypeStruct(dims, dtype)


def pack_body(nb, at_ref, x_ref, *refs):
    outs, buf = refs[:nb], refs[nb]
    width = x_ref.shape[1]
    bw = width // nb
    for j in range(0, width, LANES):
        buf[j : j + LANES, :] = x_ref[:, j : j + LANES].T
    for k in range(nb):
        start = pl.multiple_of(jnp.bitwise_xor(at_ref[0], k) * bw, 16)
        outs[k][...] = buf[pl.ds(start, bw), :]


def unpack_last_body(nb, at_ref, *refs):
    ins, own_ref = refs[:nb], refs[nb]
    token, out, sum_ref, buf = refs[nb + 1 :]
    add_last_body(own_ref, ins[nb // 2], token, sum_ref)
    unpack_body(nb, at_ref, *ins, token, out, buf)


def open_body(nb, at_ref, x_hbm, *refs):
    n = (len(refs) - nb - 3) // 2
    hbm, outs, held = refs[:n], refs[n : n + nb], refs[n + nb : 2 * n + nb]
    x_ref, buf, sems = refs[2 * n + nb :]
    copies = [pltpu.make_async_copy(x_hbm, x_ref, sems.at[0])]
    copies += [pltpu.make_async_copy(a, b, sems.at[1 + i]) for i, (a, b) in enumerate(zip(hbm, held))]
    for c in copies:
        c.start()
    copies[0].wait()
    pack_body(nb, at_ref, x_ref, *outs, buf)
    for c in copies[1:]:
        c.wait()


def unpack_body(nb, at_ref, *refs):
    ins, token, out, buf = refs[:nb], refs[nb], refs[nb + 1], refs[nb + 2]
    width = out.shape[1]
    bw = width // nb
    for k in range(nb):
        start = pl.multiple_of(jnp.bitwise_xor(at_ref[0], k) * bw, 16)
        buf[pl.ds(start, bw), :] = ins[k][0:bw, :]
    for j in range(0, width, LANES):
        out[:, j : j + LANES] = buf[j : j + LANES, :].T
    token[...] = jnp.zeros_like(token)


def prep_body(nb, n_low, at_ref, c_ref, w_ref, coef_ref, wo_ref, wt_ref, buf, table):
    levels, _, width = c_ref.shape
    bw = width // nb
    for b in range(nb):

        @pl.when(at_ref[0] == b)
        def _():
            cols = slice(b * bw, (b + 1) * bw)
            for l in range(levels):
                buf[4 * l : 4 * l + 4, :] = c_ref[l, :, cols]
            wt = w_ref[:, cols]
            wt_ref[...] = wt
            wo_ref[...] = wt.T

    row = 0
    for lower, upper, span in (
        ((0, 1, 3, 2), (3, 2, 0, 1), range(n_low, levels)),
        ((0, 1), (3, 2), range(n_low)),
        ((0, 2, 3, 1), (3, 1, 0, 2), range(n_low, levels)),
        ((0, 2), (3, 1), range(n_low)),
    ):
        for l in span:
            for a, b in zip(lower, upper):
                high = at_ref[1 + l] == 1
                i, j = 4 * l + b, 4 * l + a
                table[row : row + 1, :] = jnp.where(high, buf[i : i + 1, :], buf[j : j + 1, :])
                row += 1
    coef_ref[...] = table[...].T


def copy_body(*refs):
    n = len(refs) // 2
    for k in range(n):
        refs[n + k][...] = refs[k][...]


def mark_body(out_ref):
    out_ref[...] = jnp.zeros_like(out_ref)


def stack_body(*refs):
    out = refs[-1]
    for k, r in enumerate(refs[:-1]):
        out[k] = r[...]


def pair(coef_ref, first, s):
    return (coef_ref[s : s + CH, first : first + 1], coef_ref[s : s + CH, first + 1 : first + 2])


def combine_body(first, coef_ref, own_ref, other_ref, out_ref):
    for s in range(0, out_ref.shape[1], CH):
        c0, c1 = pair(coef_ref, first, s)
        for k in range(out_ref.shape[0]):
            own = own_ref[k, s : s + CH, :].astype(F32)
            other = other_ref[k, s : s + CH, :].astype(F32)
            out_ref[k, s : s + CH, :] = (c0 * own + c1 * other).astype(BF16)


def local_levels(vals, coef, first):
    vals = list(vals)
    nb = len(vals)
    for j in range(nb.bit_length() - 1):
        c = [coef[:, first + 4 * j + i : first + 4 * j + i + 1] for i in range(4)]
        for k in range(nb):
            if not k >> j & 1:
                m = k | 1 << j
                a, b = vals[k], vals[m]
                vals[k] = c[0] * a + c[1] * b
                vals[m] = c[2] * b + c[3] * a
    return vals


def finish_state(first, loc, coef_ref, chunks, u_ref):
    for s in range(0, u_ref.shape[1], CH):
        c0, c1 = pair(coef_ref, first, s)
        vals = []
        for own_ref, other_ref in chunks:
            for k in range(own_ref.shape[0]):
                vals.append(c0 * own_ref[k, s : s + CH, :].astype(F32) + c1 * other_ref[k, s : s + CH, :].astype(F32))
        vals = local_levels(vals, coef_ref[s : s + CH, :], loc)
        for k, v in enumerate(vals):
            u_ref[k, s : s + CH, :] = v.astype(BF16)


def mix_rows(u_ref, b_ref, ins, act_ref):
    for k, r in enumerate(ins):
        lanes = slice(k * LANES, (k + 1) * LANES)
        act_ref[:, lanes] = (r[...].astype(F32) + dot(u_ref[k], b_ref[...], 1, 1)).astype(BF16)


def forward_body(nb, first, loc, coef_ref, b_ref, wt_ref, own0, other0, own1, other1, *refs):
    ins, outs, u_ref, act_ref = refs[:nb], refs[nb : 2 * nb], refs[2 * nb], refs[2 * nb + 1]
    finish_state(first, loc, coef_ref, ((own0, other0), (own1, other1)), u_ref)
    mix_rows(u_ref, b_ref, ins, act_ref)
    act = act_ref[...]
    pre = dot(wt_ref[...], act, 1, 0)
    out = (act.astype(F32) + pre * jax.nn.sigmoid(pre)).astype(BF16)
    for k in range(nb):
        outs[k][...] = out[:, k * LANES : (k + 1) * LANES]


def backward_body(nb, first, loc, adj, coef_ref, b_ref, w_ref, wt_ref, own_ref, other_ref, *refs):
    ins, ups = refs[:nb], refs[nb : 2 * nb]
    v0_ref, v1_ref, d_ref, act_ref, gz_ref, u_ref, v_ref, up_ref = refs[2 * nb :]
    finish_state(first, loc, coef_ref, ((own_ref, other_ref),), u_ref)
    mix_rows(u_ref, b_ref, ins, act_ref)
    for k in range(nb):
        up_ref[:, k * LANES : (k + 1) * LANES] = ups[k][...]
    pre = dot(wt_ref[...], act_ref[...], 1, 0)
    sig = jax.nn.sigmoid(pre)
    gz_ref[...] = (up_ref[...].astype(F32) * (sig * (1.0 + pre * (1.0 - sig)))).astype(BF16)
    back = dot(w_ref[...], gz_ref[...], 1, 0)
    d = (up_ref[...].astype(F32) + back).astype(BF16)
    for k in range(nb):
        d_ref[k] = d[:, k * LANES : (k + 1) * LANES]
        v_ref[k] = dot(d_ref[k], b_ref[...], 1, 0)
    half = nb // 2
    for s in range(0, d_ref.shape[1], CH):
        vals = local_levels([v_ref[k, s : s + CH, :] for k in range(nb)], coef_ref[s : s + CH, :], adj)
        for k in range(half):
            v0_ref[k, s : s + CH, :] = vals[k].astype(BF16)
            v1_ref[k, s : s + CH, :] = vals[half + k].astype(BF16)


def finish_body(k0, n, first, coef_ref, own_ref, other_ref, d_ref, *outs):
    for s in range(0, own_ref.shape[1], CH):
        c0, c1 = pair(coef_ref, first, s)
        for k in range(n):
            outs[k][s : s + CH, :] = (
                d_ref[k0 + k, s : s + CH, :].astype(F32)
                + c0 * own_ref[k, s : s + CH, :].astype(F32)
                + c1 * other_ref[k, s : s + CH, :].astype(F32)
            ).astype(BF16)


def halve(at_ref, l, src, keep_ref, send_ref):
    bit = at_ref[1 + l]
    for j in range(keep_ref.shape[0]):
        keep_ref[j] = src[2 * j + bit]
        send_ref[j] = src[2 * j + 1 - bit].astype(BF16)


def grads_body(nb, act_ref, gz_ref, d_ref, u_ref, gw_ref, gb_ref):
    gw, gb = dot(act_ref[...], gz_ref[...], 1, 1), 0.0
    for k in range(nb):
        gb = gb + dot(d_ref[k], u_ref[k], 0, 0)
    gb_ref[...] = gb.astype(BF16)
    part = gw_ref.shape[1]
    for m in range(gw_ref.shape[0]):
        gw_ref[m] = gw[m * part : (m + 1) * part, :]


def join_gb_body(v_ref, gb_ref, near_ref):
    n, bw, _ = v_ref.shape
    for k in range(n):
        near_ref[k * bw : (k + 1) * bw, :] = v_ref[k]
    near_ref[n * bw :, :] = gb_ref[...]


def first_half_body(at_ref, gw_ref, keep_ref, send_ref):
    halve(at_ref, 0, gw_ref, keep_ref, send_ref)


def halve_body(l, at_ref, own_ref, other_ref, keep_ref, send_ref, buf):
    for j in range(own_ref.shape[0]):
        buf[j] = own_ref[j] + other_ref[j].astype(F32)
    halve(at_ref, l, buf, keep_ref, send_ref)


def last_body(own_ref, other_ref, token, out_ref):
    token[...] = jnp.zeros_like(token)
    out_ref[...] = own_ref[...] + other_ref[...].astype(F32)


def combine_riding_body(first, n, coef_ref, own_ref, other_ref, out_ref):
    bw = coef_ref.shape[0]
    for s in range(0, bw, CH):
        c0, c1 = pair(coef_ref, first, s)
        for k in range(n):
            r = slice(k * bw + s, k * bw + s + CH)
            out_ref[r, :] = (c0 * own_ref[r, :].astype(F32) + c1 * other_ref[r, :].astype(F32)).astype(BF16)
    r = slice(n * bw, out_ref.shape[0])
    out_ref[r, :] = (own_ref[r, :].astype(F32) + other_ref[r, :].astype(F32)).astype(BF16)


def finish_riding_body(n, first, coef_ref, own_ref, other_ref, d_ref, *outs):
    bw = coef_ref.shape[0]
    for s in range(0, bw, CH):
        c0, c1 = pair(coef_ref, first, s)
        for k in range(n):
            r = slice(k * bw + s, k * bw + s + CH)
            outs[k][s : s + CH, :] = (
                d_ref[k, s : s + CH, :].astype(F32)
                + c0 * own_ref[r, :].astype(F32)
                + c1 * other_ref[r, :].astype(F32)
            ).astype(BF16)
    r = slice(n * bw, own_ref.shape[0])
    outs[n][...] = (own_ref[r, :].astype(F32) + other_ref[r, :].astype(F32)).astype(BF16)


def join_sum_body(piece_ref, own_ref, other_ref, out_ref):
    n = piece_ref.shape[0]
    out_ref[0:n, :] = piece_ref[...]
    out_ref[n:, :] = (own_ref[...].astype(F32) + other_ref[...].astype(F32)).astype(BF16)


def add_last_body(own_ref, other_ref, token, out_ref):
    token[...] = jnp.zeros_like(token)
    r = slice(own_ref.shape[0] - out_ref.shape[0], own_ref.shape[0])
    out_ref[...] = own_ref[r, :].astype(F32) + other_ref[r, :].astype(F32)


class Chain:
    def __init__(self):
        self.last = []

    def __call__(self, *args, deps=(), **kwargs):
        outs = call(*args, deps=[*self.last, *deps], declared=STEP, **kwargs)
        self.last = [jax.tree.leaves(outs)[0]]
        return outs


def on_device(prev_out, prev_grad, saved_in, seq_mix, coeffs, mixer):
    n_sec, n_seq = lax.axis_size("section"), lax.axis_size("seq")
    weights = mixer[0]
    width, bw = weights.shape
    nb = width // bw
    low = n_seq // nb
    levels = n_seq.bit_length() - 1
    n_low = low.bit_length() - 1
    n_top = levels - n_low
    q = lax.axis_index("seq").astype(jnp.int32)
    at = jnp.stack([q // low] + [jnp.bitwise_and(jnp.right_shift(q, l), 1) for l in range(levels)])
    rows = prev_out.shape[1]
    half = nb // 2
    fwd_loc, fwd_low = 0, 4 * n_top
    adj_loc = fwd_low + 2 * n_low
    adj_low = adj_loc + 4 * n_top
    n_coef = adj_low + 2 * n_low

    def send(x, shift, flip, name="p"):
        with jax.named_scope(name):
            return send_(x, shift, flip)

    def send_(x, shift, flip):
        pairs = [
            (s * n_seq + i, (s + shift) % n_sec * n_seq + (i ^ flip)) for s in range(n_sec) for i in range(n_seq)
        ]
        return lax.ppermute(x, ("section", "seq"), pairs)

    run = Chain()

    def pack(x, name, deps=()):
        return run(
            functools.partial(pack_body, nb),
            [shape(bw, rows)] * nb,
            [at, x],
            [pltpu.VMEM((width, rows), BF16)],
            name,
            deps=deps,
        )

    token = shape(8, LANES, dtype=F32)

    def unpack(pieces, name):
        return run(
            functools.partial(unpack_body, nb),
            [token, shape(rows, width)],
            [at, *[pieces[k] for k in range(nb)]],
            [pltpu.VMEM((width, rows), BF16)],
            name,
            out_hbm=True,
        )[1]

    def release(pieces, name, deps=()):
        return run(copy_body, [shape(*p.shape) for p in pieces], pieces, (), name, deps=deps)

    def stack(pieces, name, deps=()):
        return run(stack_body, shape(len(pieces), bw, rows), pieces, (), name, deps=deps)

    def beside(u, work):
        return call(mark_body, shape(8, LANES, dtype=F32), [], (), "mark", [u], declared=work)

    def cross(u, flip, name):
        if name in ("fn_level1", "ff_level1", "s_level1", "d_far_level1", "d_near_level1", "sum_w0"):
            return send(u, 0, flip, name), u
        mark = call(mark_body, shape(8, LANES, dtype=F32), [], (), "mark", [u], declared=11500 * u.size * 2)
        return send(u, 0, flip, name), mark

    def open_step(u, name):
        return u, *cross(u, 1, f"{name}_level0")

    def more_steps(opened, first, name, deps=()):
        u, other, mark = opened
        for l in range(1, n_low):
            u = run(
                functools.partial(combine_body, first + 2 * (l - 1)),
                shape(*u.shape),
                [coef, u, other],
                (),
                f"mix_{name}",
                deps=[mark, *deps],
            )
            other, mark = cross(u, 1 << l, f"{name}_level{l}")
        return u, other, mark

    far = range(half, nb)
    far_first = [*reversed(far), *reversed(range(1, half))]

    def spread(pieces, shift, ks, name):
        return {k: send(pieces[k], shift, k * low, f"{name}{k}") for k in ks}

    def fetch(x, held, name):
        return run(
            functools.partial(open_body, nb),
            [shape(bw, rows)] * nb + [shape(*a.shape, dtype=a.dtype) for a in held],
            [at],
            [
                pltpu.VMEM((rows, width), BF16),
                pltpu.VMEM((width, rows), BF16),
                pltpu.SemaphoreType.DMA((1 + len(held),)),
            ],
            name,
            in_hbm=[x, *held],
        )

    sp = fetch(saved_in[0], [], "pack_s")
    sr = {0: sp[0], **spread(sp, 0, range(1, nb), "in_s")}
    *up, incoming, factors, w_t, blocks = fetch(
        prev_grad[0], [prev_out[0], coeffs[0], weights.T, seq_mix[0]], "pack_u"
    )
    ur = spread(up, -1, [*reversed(range(half)), *far[:-1]], "in_u")
    coef, w_own, w_own_t = run(
        functools.partial(prep_body, nb, n_low),
        [shape(bw, n_coef, dtype=F32), shape(bw, bw), shape(bw, bw)],
        [at, factors, w_t],
        [pltpu.VMEM((4 * levels, bw), F32), pltpu.VMEM((n_coef, bw), F32)],
        "prep",
        deps=[sr[1]],
    )
    s_open = open_step(stack([sr[k] for k in range(nb)], "stack_s"), "s")
    fp = pack(incoming, "pack_f")
    s_all = more_steps(s_open, fwd_low, "s", [ur[k] for k in range(half)])
    fr = spread(fp, 1, reversed(range(half)), "in_f")
    ur[nb - 1] = spread({nb - 1: release(up[nb - 1 :], "release_u", [ur[half]])[0]}, -1, [nb - 1], "in_u")[nb - 1]
    f_far = release(fp[half:], "release_f", [ur[nb - 1]])
    fr.update(spread(dict(zip(far, f_far)), 1, far, "in_f"))
    near_open = open_step(stack([fr[k] for k in range(half)], "stack_fn"), "fn")
    fn = more_steps(near_open, fwd_low, "fn")

    f_last = fwd_low + 2 * (n_low - 1)
    a_last = adj_low + 2 * (n_low - 1)
    v_near, v_far, d, act, gz, u = run(
        functools.partial(backward_body, nb, f_last, fwd_loc, adj_loc),
        [shape(half, bw, rows), shape(nb - half, bw, rows), shape(nb, bw, rows)]
        + [shape(bw, nb * rows)] * 2
        + [shape(nb, bw, rows)],
        [
            coef,
            blocks,
            w_own,
            w_own_t,
            *s_all[:2],
            *[sr[k] for k in range(nb)],
            *[ur[k] for k in range(nb)],
        ],
        [pltpu.VMEM((nb, bw, rows), F32), pltpu.VMEM((bw, nb * rows), BF16)],
        "layer_b",
        deps=[s_all[2]],
    )
    far_open = open_step(v_far, "d_far")
    part = bw // low
    gw, gb = run(
        functools.partial(grads_body, nb),
        [shape(low, part, bw, dtype=F32), shape(rows, rows)],
        [act, gz, d, u],
        (),
        "weight_grads",
    )
    near = run(join_gb_body, shape(half * bw + rows, rows), [v_near, gb], (), "join_near")
    own, other, mark_n = open_step(near, "d_near")
    keep, give = run(
        first_half_body,
        [shape(low // 2, part, bw, dtype=F32), shape(low // 2, part, bw)],
        [at, gw],
        (),
        "sum_w",
    )
    got, mark = cross(give, 1, "sum_w0")
    d_far = more_steps(far_open, adj_low, "d_far")
    for l in range(1, n_low):
        own = run(
            functools.partial(combine_riding_body, adj_low + 2 * (l - 1), half),
            shape(*near.shape),
            [coef, own, other],
            (),
            "mix_d_near",
            deps=[mark_n],
        )
        other, mark_n = cross(own, 1 << l, f"d_near_level{l}")
    d_near = own, other, mark_n
    ff = more_steps(open_step(stack([fr[k] for k in far], "stack_ff"), "ff"), fwd_low, "ff", [fn[1]])
    own, other, ready = d_far
    outs = run(
        functools.partial(finish_body, half, nb - half, a_last),
        [shape(bw, rows)] * (nb - half),
        [coef, own, other, d],
        (),
        "finish_far",
        deps=[ready],
    )
    od = spread(dict(zip(far, outs)), 0, reversed(far), "out_d")
    for l in range(n_low - 1):
        m = low >> l + 2
        keep, give = run(
            functools.partial(halve_body, l + 1),
            [shape(m, part, bw, dtype=F32), shape(m, part, bw)],
            [at, keep, got],
            [pltpu.VMEM((2 * m, part, bw), F32)],
            "sum_w",
            deps=[mark],
        )
        got, mark = cross(give, 2 << l, f"sum_w{l + 1}")
    own, other, ready = d_near
    outs = run(
        functools.partial(finish_riding_body, half, a_last),
        [shape(bw, rows)] * half + [shape(rows, rows)],
        [coef, own, other, d],
        (),
        "finish_near",
        deps=[ready],
    )
    *outs, gb = outs
    od[0] = outs[0]
    od.update(spread(dict(enumerate(outs)), 0, range(1, half), "out_d"))
    got_b, mark_b = cross(gb, low, "sum_b0")
    fo = run(
        functools.partial(forward_body, nb, f_last, fwd_loc),
        [shape(bw, rows)] * nb,
        [coef, blocks, w_own_t, *fn[:2], *ff[:2], *[fr[k] for k in range(nb)]],
        [pltpu.VMEM((nb, bw, rows), BF16), pltpu.VMEM((bw, nb * rows), BF16)],
        "layer_f",
        deps=[fn[2], ff[2]],
    )
    of = {0: fo[0], **spread(fo, 0, [k for k in far_first if k != half], "out_f")}
    last_piece = run(
        join_sum_body,
        shape(bw + rows, rows),
        [fo[half], gb, got_b],
        (),
        "join_f",
        deps=[mark_b, od[nb - 1]],
    )
    of[half] = send(last_piece, 0, half * low, f"out_f{half}")
    out_d = unpack(od, "unpack_d")
    _, grad_w = run(
        last_body,
        [token, shape(1, part, bw, dtype=F32)],
        [keep, got],
        (),
        "sum_w",
        deps=[mark],
        out_hbm=True,
    )
    _, out_f, grad_b = run(
        functools.partial(unpack_last_body, nb),
        [token, shape(rows, width), shape(rows, rows, dtype=F32)],
        [at, *[of[k] for k in range(nb)], last_piece],
        [pltpu.VMEM((width, rows), BF16)],
        "unpack_f",
        out_hbm=True,
    )
    return out_f[None], out_d[None], grad_w, grad_b[None]


def solution(mesh):
    placed = (
        P("section", "seq", None),
        P("section", "seq", None),
        P("section", "seq", None),
        P("section", None, None),
        P("section", None, None, None),
        P("section", None, None),
    )
    return jax.shard_map(
        on_device,
        mesh=mesh,
        in_specs=placed,
        out_specs=(
            P("section", "seq", None),
            P("section", "seq", None),
            P("section", "seq", None),
            P("section", None, None),
        ),
        check_vma=False,
    )
```
